32 devices in a mesh: shard: 4 (over y, x), ctx: 2 (over core), tp: 4 (over z).
Axes of the slice: x: 2, y: 2, z: 4, core: 2. Of those that a mesh axis runs over, the one named last changes fastest.
Arguments:
- hidden_in: bfloat16 [16, 1024, 768], P('shard', ('ctx', 'tp')), may hold values from -6 to 6
- norm_attn_gain: float32 [768], replicated, may hold values from 0.5 to 1.5
- query_weight: bfloat16 [768, 768], P('shard', 'tp'), may hold values from -0.0546875 to 0.0546875
- key_weight: bfloat16 [768, 768], P('shard', 'tp'), may hold values from -0.21875 to 0.21875
- value_weight: bfloat16 [768, 768], P('shard', 'tp'), may hold values from -0.21875 to 0.21875
- out_weight: bfloat16 [768, 768], P(('tp', 'shard')), may hold values from -1.25 to 1.25
- bias_table: float32 [32, 12], replicated, may hold values from -4 to 4
- norm_ffn_gain: float32 [768], replicated, may hold values from 0.5 to 1.5
- ffn_in_weight: bfloat16 [768, 3072], P('shard', 'tp'), may hold values from -0.21875 to 0.21875
- ffn_out_weight: bfloat16 [3072, 768], P(('tp', 'shard')), may hold values from -0.109375 to 0.109375
- buckets: int32 [1024, 1024], P('ctx'), may hold values from 0 to 31
- output_gradient: bfloat16 [16, 1024, 768], P('shard', ('ctx', 'tp')), may hold values from -16 to 16
Outputs:
- hidden_out: bfloat16 [16, 1024, 768], P('shard', ('ctx', 'tp'))
- hidden_grad: float32 [16, 1024, 768], P('shard', ('ctx', 'tp'))
- attention_norm_gain_gradient: float32 [768], replicated
- query_weight_grad: float32 [768, 768], P('shard', 'tp')
- key_weight_grad: float32 [768, 768], P('shard', 'tp')
- value_weight_grad: float32 [768, 768], P('shard', 'tp')
- out_weight_grad: float32 [768, 768], P(('tp', 'shard'))
- bias_table_grad: float32 [32, 12], replicated
- norm_ffn_gain_grad: float32 [768], replicated
- ffn_in_weight_grad: float32 [768, 3072], P('shard', 'tp')
- ffn_out_weight_grad: float32 [3072, 768], P(('tp', 'shard'))
The draws below stay inside these ranges and needn't reach their ends.
All inputs are finite; a program needn't handle non-finite values.
Results may differ from the reference program's by a relative error of at most 0.018.
Values may be sent and summed in bfloat16 or wider, within the bound.
No kernel may reach another device: no remote copies, remote signals or barrier semaphores. Data moves between devices by JAX's collectives and lax.ppermute only.
A program may use at most 192 MiB of HBM per device.

```python
import math
from functools import partial
import jax
import jax.numpy as jnp
from jax import lax

D = 768
HEADS = 12
FF = 3072
BUCKETS = 32
LEN = 1024
SEQS = 16


def draw_output_gradient(key, part):
    row_total = SEQS * LEN
    place = (jnp.arange(SEQS, dtype=jnp.float32)[:, None] * LEN + jnp.arange(LEN, dtype=jnp.float32)[None, :]) / (row_total - 1)
    base = jnp.clip(jax.random.normal(key, (SEQS, LEN, D), jnp.float32), -4.0, 4.0)
    growth = jnp.exp(place * math.log(3.0))
    return (base * growth[:, :, None]).astype(jnp.bfloat16)


def touch_ends(result, key, least, high):
    spot = [jax.random.randint(jax.random.fold_in(key, axis), (), 0, length) for axis, length in enumerate(result.shape)]
    widest = result.shape.index(max(result.shape))
    next_to = spot[:widest] + [(spot[widest] + 1) % result.shape[widest]] + spot[widest + 1:]
    return result.at[tuple(spot)].set(least).at[tuple(next_to)].set(high)


def steps_of(key, shape, split, low, largest):
    def one(axis_at, shards_of):
        steps = jax.random.uniform(jax.random.fold_in(jax.random.fold_in(key, 6), axis_at), (shards_of,), jnp.float32, low / len(split), largest / len(split))
        return jnp.repeat(jnp.exp(steps), shape[axis_at] // shards_of).reshape((-1,) + (1,) * (len(shape) - axis_at - 1))

    factor_of = one(*split[0])
    for cut in split[1:]:
        factor_of = factor_of * one(*cut)
    return factor_of


def gaussian(rng, extent, scale, reach, pieces=(), kind=jnp.bfloat16):
    values = scale * jax.random.normal(rng, extent, jnp.float32)
    if pieces:
        values = values * steps_of(rng, extent, pieces, -0.22, 0.18)
    return jnp.clip(values, -reach, reach).astype(kind)


def setup_inputs(seed: int = 0) -> dict:
    keys = jax.random.split(jax.random.key(seed), 13)
    hidden_in = gaussian(keys[0], (SEQS, LEN, D), 1.0, 6.0, ((0, 4), (1, 8)))
    norm_attn_gain = jnp.clip(1.0 + 0.1 * jax.random.normal(keys[1], (D,), jnp.float32), 0.5, 1.5)
    query_weight = gaussian(keys[2], (D, D), (D * 16) ** -0.5, 0.0546875, ((0, 4), (1, 4)))
    key_weight = gaussian(keys[3], (D, D), D ** -0.5, 0.21875, ((0, 4), (1, 4)))
    value_weight = gaussian(keys[4], (D, D), D ** -0.5, 0.21875, ((0, 4), (1, 4)))
    out_weight = gaussian(keys[5], (D, D), (D // 32) ** -0.5, 1.25, ((0, 16),))
    bias_table = gaussian(keys[6], (BUCKETS, HEADS), 1.0, 4.0, (), jnp.float32)
    norm_ffn_gain = jnp.clip(1.0 + 0.1 * jax.random.normal(keys[7], (D,), jnp.float32), 0.5, 1.5)
    ffn_in_weight = gaussian(keys[8], (D, FF), D ** -0.5, 0.21875, ((0, 4), (1, 4)))
    ffn_out_weight = gaussian(keys[9], (FF, D), FF ** -0.5, 0.109375, ((0, 16),))
    buckets = touch_ends(jax.random.randint(keys[10], (LEN, LEN), 0, BUCKETS), jax.random.fold_in(keys[10], 1), 0, BUCKETS - 1).astype(jnp.int32)
    output_gradient = draw_output_gradient(jax.random.fold_in(keys[12], 71), 0)
    return dict(hidden_in=hidden_in, norm_attn_gain=norm_attn_gain, query_weight=query_weight, key_weight=key_weight, value_weight=value_weight, out_weight=out_weight, bias_table=bias_table, norm_ffn_gain=norm_ffn_gain, ffn_in_weight=ffn_in_weight, ffn_out_weight=ffn_out_weight, buckets=buckets, output_gradient=output_gradient)


@jax.custom_vjp
def low(v):
    return lax.optimization_barrier(v.astype(jnp.bfloat16)).astype(jnp.float32)

@jax.custom_vjp
def low_back(v):
    return v

def low_keep(v):
    return (low(v), None)

def low_pass(kept, grad):
    return (grad,)

def back_keep(v):
    return (v, None)

def back_low(kept, grad):
    return (low(grad),)
low.defvjp(low_keep, low_pass)
low_back.defvjp(back_keep, back_low)

def rms_norm(values, gain_vec):
    return values * lax.rsqrt(lax.optimization_barrier(jnp.mean(values * values, axis=-1, keepdims=True)) + 1e-06) * gain_vec

def matmul_high(left_side, right_side):
    return jnp.matmul(left_side, right_side, precision=lax.Precision.HIGHEST)

def smooth_units(values):
    return jax.nn.gelu(values, approximate=True)

def attend_one(pos_bias, triple):
    query_seq, key_seq, value_seq = triple
    head_size = D // HEADS
    q_heads = query_seq.reshape(LEN, HEADS, head_size)
    k_heads = key_seq.reshape(LEN, HEADS, head_size)
    v_heads = value_seq.reshape(LEN, HEADS, head_size)
    scores = jnp.einsum('qhd,khd->hqk', q_heads, k_heads, precision=lax.Precision.HIGHEST) + pos_bias
    scores = low_back(scores)
    prob_low = low(jax.nn.softmax(scores, axis=-1))
    mixed_out = jnp.einsum('hqk,khd->qhd', prob_low, v_heads, precision=lax.Precision.HIGHEST)
    return mixed_out.reshape(LEN, D)

def layer(buckets, source, params):
    attn_gain, w_query, w_key, w_value, w_out, table, ffn_gain, w_first, w_second = params
    normed_attn = low(rms_norm(source, attn_gain))
    query_rows = low_back(low(matmul_high(normed_attn, w_query)))
    key_rows = low_back(low(matmul_high(normed_attn, w_key)))
    value_rows = low_back(low(matmul_high(normed_attn, w_value)))
    pos_bias = jnp.transpose(jnp.take(table, buckets, axis=0), (2, 0, 1))
    attended = lax.map(jax.checkpoint(partial(attend_one, pos_bias)), (query_rows, key_rows, value_rows))
    attended = low_back(low(attended))
    middle = source + low_back(matmul_high(attended, w_out))
    normed_ffn = low(rms_norm(middle, ffn_gain))
    pre_units = low_back(matmul_high(normed_ffn, w_first))
    units_low = low(smooth_units(pre_units))
    return middle + low_back(matmul_high(units_low, w_second))

def reference(hidden_in, norm_attn_gain, query_weight, key_weight, value_weight, out_weight, bias_table, norm_ffn_gain, ffn_in_weight, ffn_out_weight, buckets, output_gradient):
    params = (norm_attn_gain.astype(jnp.float32), query_weight.astype(jnp.float32), key_weight.astype(jnp.float32), value_weight.astype(jnp.float32), out_weight.astype(jnp.float32), bias_table.astype(jnp.float32), norm_ffn_gain.astype(jnp.float32), ffn_in_weight.astype(jnp.float32), ffn_out_weight.astype(jnp.float32))
    group_size = 4
    group_count = SEQS // group_size
    inputs = hidden_in.astype(jnp.float32).reshape(group_count, group_size, LEN, D)
    cotangents = output_gradient.astype(jnp.float32).reshape(group_count, group_size, LEN, D)
    layer_fixed = partial(layer, buckets)
    zero_grads = jax.tree.map(jnp.zeros_like, params)

    def step(totals, pair_items):
        source, cotangent = pair_items
        output, pull_back = jax.vjp(layer_fixed, source, params)
        source_grad, param_grads = pull_back(cotangent)
        totals = jax.tree.map(jnp.add, totals, param_grads)
        return (totals, (output.astype(jnp.bfloat16), source_grad))
    totals, (outputs, source_grads) = lax.scan(step, zero_grads, (inputs, cotangents))
    hidden_out = outputs.reshape(SEQS, LEN, D)
    hidden_grad = source_grads.reshape(SEQS, LEN, D)
    return (hidden_out, hidden_grad, totals[0], totals[1], totals[2], totals[3], totals[4], totals[5], totals[6], totals[7], totals[8])
```

```python
from functools import partial

import jax
import jax.numpy as jnp
from jax import lax
from jax.experimental import pallas as pl
from jax.experimental.pallas import tpu as pltpu
from jax.sharding import PartitionSpec as P

EPS = 1e-06
F32 = jnp.float32
BF = jnp.bfloat16
ALL = ("shard", "ctx", "tp")
NN = (((1,), (0,)), ((), ()))
NT = (((1,), (1,)), ((), ()))
TN = (((0,), (0,)), ((), ()))
BIG = 56 * 1024 * 1024


def dot(a, b, dims=NN):
    return lax.dot_general(a, b, dims, preferred_element_type=F32)


def call(kernel, out_shape, name, grid=None, in_specs=None, out_specs=None, scratch=(), prefetch=0, aliases=None):
    kwargs = {}
    if grid is None:
        grid = (1,)
    if in_specs is not None:
        kwargs["in_specs"] = in_specs
    if out_specs is not None:
        kwargs["out_specs"] = out_specs
    return pl.pallas_call(
        kernel,
        out_shape=out_shape,
        grid_spec=pltpu.PrefetchScalarGridSpec(
            num_scalar_prefetch=prefetch, grid=grid, scratch_shapes=scratch, **kwargs
        ),
        compiler_params=pltpu.CompilerParams(vmem_limit_bytes=BIG),
        input_output_aliases=aliases or {},
        name=name,
    )


def whole(*shape):
    return pl.BlockSpec(shape, lambda *_: (0,) * len(shape))


def sds(shape, dtype):
    return jax.ShapeDtypeStruct(shape, dtype)


def bias_kernel(place, table_ref, buckets_ref, out_ref):
    tp = place[0]
    heads = table_ref.shape[0]
    blocks = out_ref.shape[2] // 128
    for k in range(blocks):
        start = pl.multiple_of((tp ^ k) * 128, 128)
        index = buckets_ref[:, pl.ds(start, 128)]
        for h in range(heads):
            row = jnp.broadcast_to(table_ref[h : h + 1, :], index.shape)
            out_ref[h, :, 128 * k : 128 * k + 128] = jnp.take_along_axis(row, index, axis=1)


def position_bias(place, table_rel, buckets_t):
    heads = table_rel.shape[0]
    keys, queries = buckets_t.shape
    per_half = keys // 256

    def source(j, place):
        return ((place[1] ^ (j // per_half)) * per_half + (place[0] ^ (j % per_half)), 0)

    return call(
        bias_kernel,
        sds((heads, keys, queries), F32),
        "position_bias",
        grid=(keys // 128,),
        in_specs=[pl.BlockSpec((heads, 128), lambda j, p: (0, 0)), pl.BlockSpec((128, queries), source)],
        out_specs=pl.BlockSpec((heads, 128, queries), lambda j, p: (0, j, 0)),
        prefetch=1,
    )(place, table_rel, buckets_t)


def qkv_kernel(place, x0, x1, x2, x3, gain, mine, other, x_out, xn_out, q_out, k_out, v_out, a_out, o_out):
    first = place[1] == 0
    for r, ref in enumerate((x0, x1, x2, x3)):
        x = ref[...]
        x_out[128 * r : 128 * r + 128, :] = x
        xf = x.astype(F32)
        scale = lax.rsqrt(jnp.mean(xf * xf, axis=-1, keepdims=True) + EPS)
        xn_out[128 * r : 128 * r + 128, :] = (xf * scale * gain[...]).astype(BF)
    for k in range(4):
        for s in range(4):
            m = mine[place[2 + s], k]
            o = other[place[6 + s], k]
            a_out[k, 192 * s : 192 * s + 192, 0:384] = jnp.where(first, m, o)
            a_out[k, 192 * s : 192 * s + 192, 384:768] = jnp.where(first, o, m)
        for s in range(4):
            for c in range(4):
                o_out[192 * k + 48 * s : 192 * k + 48 * s + 48, 192 * c : 192 * c + 192] = a_out[
                    k, 192 * s + 48 * c : 192 * s + 48 * c + 48, 576:768
                ]
        y = dot(xn_out[...], a_out[k, :, 0:576]).astype(BF)
        q_out[:, 192 * k : 192 * k + 192] = y[:, 0:192]
        k_out[:, 192 * k : 192 * k + 192] = y[:, 192:384]
        v_out[:, 192 * k : 192 * k + 192] = y[:, 384:576]


def attend_kernel(q_ref, k0_ref, v0_ref, k1_ref, v1_ref, bias_ref, att_ref, full_ref, lse_ref):
    lane = lax.broadcasted_iota(jnp.int32, (1, 128), 1)
    keys = k0_ref.shape[0]
    result = None
    for h in range(2):
        keep = (lane < 64) if h == 0 else (lane >= 64)
        q = jnp.where(keep, q_ref[...], jnp.zeros((), BF))
        s0 = dot(k0_ref[...], q, NT) + bias_ref[h, 0:keys, :]
        s1 = dot(k1_ref[...], q, NT) + bias_ref[h, keys : 2 * keys, :]
        top = jnp.maximum(jnp.max(s0, axis=0, keepdims=True), jnp.max(s1, axis=0, keepdims=True))
        e0 = jnp.exp(s0 - top)
        e1 = jnp.exp(s1 - top)
        total = jnp.sum(e0, axis=0, keepdims=True) + jnp.sum(e1, axis=0, keepdims=True)
        lse_ref[0, h : h + 1, :] = top + jnp.log(total)
        inverse = 1.0 / total
        p0 = (e0 * inverse).astype(BF)
        p1 = (e1 * inverse).astype(BF)
        part = dot(p0, v0_ref[...], TN) + dot(p1, v1_ref[...], TN)
        result = part if h == 0 else jnp.where(keep, part, result)
    full_ref[...] = result
    att_ref[...] = result.astype(BF)


def attend(q, k0, v0, k1, v1, bias):
    rows, width = q.shape
    pairs = width // 128
    keys = bias.shape[1]
    col = pl.BlockSpec((rows, 128), lambda p: (0, p))
    return call(
        attend_kernel,
        (sds((rows, width), BF), sds((rows, width), F32), sds((pairs, 2, rows), F32)),
        "attend",
        grid=(pairs,),
        in_specs=[col] * 5 + [pl.BlockSpec((2, keys, rows), lambda p: (p, 0, 0))],
        out_specs=(col, col, pl.BlockSpec((1, 2, rows), lambda p: (p, 0, 0))),
    )(q, k0, v0, k1, v1, bias)


def project_kernel(x_ref, att_ref, o_ref, gain, mid_ref, nf_ref):
    mid = x_ref[...].astype(F32) + dot(att_ref[...], o_ref[...])
    mid_ref[...] = mid
    scale = lax.rsqrt(jnp.mean(mid * mid, axis=-1, keepdims=True) + EPS)
    nf_ref[...] = (mid * scale * gain[...]).astype(BF)


def ffn_kernel(first_call, place, nf_ref, g0, g1, g2, g3, w1m, w1o, w2m, w2o, *refs):
    if first_call:
        out_ref, dnf_ref, keep1, keep2, send1, send2, w1s, w2s, gs = refs
    else:
        out_in, dnf_in, out_ref, dnf_ref, keep1, keep2, send1, send2, w1s, w2s, gs = refs
    first = place[1] == 0
    for r, ref in enumerate((g0, g1, g2, g3)):
        gs[128 * r : 128 * r + 128, :] = ref[...]
    for s in range(4):
        rows = slice(192 * s, 192 * s + 192)
        for a, b, w in ((w1m, w1o, w1s), (w2m, w2o, w2s)):
            m = a[place[2 + s], 0]
            o = b[place[6 + s], 0]
            w[rows, 0:384] = jnp.where(first, m, o)
            w[rows, 384:768] = jnp.where(first, o, m)
    nf = nf_ref[...]
    g = gs[...]
    v = dot(nf, w1s[...])
    square = v * v
    th = jnp.tanh(0.7978845608 * (v + 0.044715 * v * square))
    half = 0.5 * (1.0 + th)
    units = (v * half).astype(BF)
    slope = half + 0.5 * v * (1.0 - th * th) * (0.7978845608 * (1.0 + 3 * 0.044715 * square))
    d_pre = (dot(g, w2s[...], NT) * slope).astype(BF)
    if first_call:
        out_ref[...] = dot(units, w2s[...])
        dnf_ref[...] = dot(d_pre, w1s[...], NT)
    else:
        out_ref[...] = out_in[...] + dot(units, w2s[...])
        dnf_ref[...] = dnf_in[...] + dot(d_pre, w1s[...], NT)
    d1 = dot(nf, d_pre, TN).astype(BF)
    d2 = dot(units, g, TN).astype(BF)
    for s in range(4):
        rows = slice(192 * s, 192 * s + 192)
        for d, keep, send in ((d1, keep1, send1), (d2, keep2, send2)):
            lo = d[rows, 0:384]
            hi = d[rows, 384:768]
            keep[place[2 + s]] = jnp.where(first, lo, hi)
            send[place[6 + s]] = jnp.where(first, hi, lo)


def ffn_block(k, place, nf, g, w1m, w1o, w2m, w2o, carry):
    rows, width = nf.shape
    acc = whole(rows, width)
    wspec = pl.BlockSpec((4, 1, 192, 384), lambda i, p: (0, k, 0, 0))
    gspec = whole(4, 192, 384)
    first = carry is None
    ins = [place, nf, *g, w1m, w1o, w2m, w2o] + ([] if first else list(carry))
    return call(
        partial(ffn_kernel, first),
        (sds((rows, width), F32), sds((rows, width), F32)) + (sds((4, 192, 384), BF),) * 4,
        "ffn",
        in_specs=[acc] + [whole(128, width)] * 4 + [wspec] * 4 + ([] if first else [acc, acc]),
        out_specs=(acc, acc, gspec, gspec, gspec, gspec),
        scratch=[pltpu.VMEM((768, 768), BF), pltpu.VMEM((768, 768), BF), pltpu.VMEM((rows, width), BF)],
        prefetch=1,
    )(*ins)


def turn_kernel(mid_ref, out_in, dnf_in, g0, g1, g2, g3, gain, o_ref, full_ref, hid_ref, dmid_ref, dml_ref, da_ref, delta_ref, gg_ref):
    mid = mid_ref[...]
    hid_ref[...] = (mid + out_in[...]).astype(BF)
    scale = lax.rsqrt(jnp.mean(mid * mid, axis=-1, keepdims=True) + EPS)
    up = dnf_in[...]
    weighted = up * gain[...]
    mean_term = jnp.mean(weighted * mid, axis=-1, keepdims=True)
    res = scale * weighted - mid * (scale * scale * scale) * mean_term
    gg_ref[...] = jnp.sum(up * mid * scale, axis=0, keepdims=True)
    for r, ref in enumerate((g0, g1, g2, g3)):
        rows = slice(128 * r, 128 * r + 128)
        dmid_ref[rows, :] = res[rows, :] + ref[...].astype(F32)
    low = dmid_ref[...].astype(BF)
    dml_ref[...] = low
    da = dot(low, o_ref[...], NT).astype(BF)
    da_ref[...] = da
    heads = delta_ref.shape[0]
    width = da.shape[1]
    head = lax.broadcasted_iota(jnp.int32, (heads, width), 0)
    lane = lax.broadcasted_iota(jnp.int32, (heads, width), 1)
    pick = jnp.where(lane // 64 == head, 1.0, 0.0)
    delta_ref[...] = lax.dot_general(
        pick, da.astype(F32) * full_ref[...], NT, precision=lax.Precision.HIGHEST, preferred_element_type=F32
    )


def attend_back_kernel(last, q_ref, da_ref, k_ref, v_ref, bias_ref, lse_ref, delta_ref, *refs):
    if last:
        dq_in, dq_ref, dk_ref, dv_ref, ds_ref = refs
    else:
        dq_ref, dk_ref, dv_ref, ds_ref = refs
    lane = lax.broadcasted_iota(jnp.int32, (1, 128), 1)
    k = k_ref[...]
    v = v_ref[...]
    dq = dk = dv = None
    zero = jnp.zeros((), BF)
    for h in range(2):
        keep = (lane < 64) if h == 0 else (lane >= 64)
        q = jnp.where(keep, q_ref[...], zero)
        da = jnp.where(keep, da_ref[...], zero)
        p = jnp.exp(dot(k, q, NT) + bias_ref[h] - lse_ref[0, h : h + 1, :])
        dp = dot(v, da, NT)
        ds = (p * (dp - delta_ref[0, h : h + 1, :])).astype(BF)
        ds_ref[h] = ds
        a = dot(ds, jnp.where(keep, k, zero), TN)
        b = dot(ds, q)
        c = dot(p.astype(BF), da)
        dq, dk, dv = (a, b, c) if h == 0 else (dq + a, dk + b, dv + c)
    dk_ref[...] = dk.astype(dk_ref.dtype)
    dv_ref[...] = dv.astype(dv_ref.dtype)
    if last:
        dq_ref[...] = (dq_in[...] + dq).astype(dq_ref.dtype)
    else:
        dq_ref[...] = dq


def attend_back(half, q, da, k, v, bias, lse, delta, dq):
    rows, width = q.shape
    pairs = width // 128
    keys = k.shape[0]
    col = pl.BlockSpec((rows, 128), lambda p: (0, p))
    stat = pl.BlockSpec((1, 2, rows), lambda p: (p, 0, 0))
    last = dq is not None
    return call(
        partial(attend_back_kernel, last),
        (
            sds((rows, width), BF if last else F32),
            sds((keys, width), F32 if last else BF),
            sds((keys, width), F32 if last else BF),
            sds((2 * pairs, keys, rows), BF),
        ),
        "attend_back",
        grid=(pairs,),
        in_specs=[col] * 4 + [pl.BlockSpec((2, keys, rows), lambda p: (p, half, 0)), stat, stat] + ([col] if last else []),
        out_specs=(col, col, col, pl.BlockSpec((2, keys, rows), lambda p: (p, 0, 0))),
    )(*([q, da, k, v, bias, lse, delta] + ([dq] if last else [])))


def weights_kernel(place, xn_ref, dq_ref, dk_in, dv_in, dk_add, dv_add, a_ref, att_ref, dml_ref, dmid_ref, x_ref, gain, keep, send, back_ref, gg_ref):
    first = place[1] == 0
    dq = dq_ref[...]
    dk = (dk_in[...] + dk_add[...].astype(F32)).astype(BF)
    dv = (dv_in[...] + dv_add[...].astype(F32)).astype(BF)
    xn = xn_ref[...]
    up = None
    for k in range(4):
        cols = slice(192 * k, 192 * k + 192)
        cat = jnp.concatenate([dq[:, cols], dk[:, cols], dv[:, cols]], axis=1)
        part = dot(cat, a_ref[k, :, 0:576], NT)
        up = part if k == 0 else up + part
        grad = dot(xn, cat, TN).astype(BF)
        out = dot(att_ref[:, cols], dml_ref[...], TN).astype(BF)
        for s in range(4):
            rows = slice(192 * s, 192 * s + 192)
            lo = grad[rows, 0:384]
            piece = jnp.concatenate(
                [out[48 * s : 48 * s + 48, 192 * c : 192 * c + 192] for c in range(4)], axis=0
            )
            hi = jnp.concatenate([grad[rows, 384:576], piece], axis=1)
            keep[place[2 + s], k] = jnp.where(first, lo, hi)
            send[place[6 + s], k] = jnp.where(first, hi, lo)
    x = x_ref[...].astype(F32)
    scale = lax.rsqrt(jnp.mean(x * x, axis=-1, keepdims=True) + EPS)
    weighted = up * gain[...]
    mean_term = jnp.mean(weighted * x, axis=-1, keepdims=True)
    res = scale * weighted - x * (scale * scale * scale) * mean_term
    gg_ref[...] = jnp.sum(up * x * scale, axis=0, keepdims=True)
    back_ref[...] = (dmid_ref[...] + res).astype(BF)


def bucket_kernel(place, buckets_ref, ds_ref, out_ref, acc, table):
    tp = place[0]
    step = pl.program_id(0)
    heads, group, queries = ds_ref.shape
    blocks = queries // 128

    @pl.when(step == 0)
    def _():
        acc[...] = jnp.zeros_like(acc)

    label = lax.broadcasted_iota(jnp.int32, (32, 128), 0)
    for g in range(group // 16):
        for k in range(blocks):
            start = pl.multiple_of((tp ^ k) * 128, 128)
            index = buckets_ref[16 * g : 16 * g + 16, pl.ds(start, 128)]
            for j in range(16):
                hit = index[j : j + 1, :] == label
                table[32 * j : 32 * j + 32, 128 * k : 128 * k + 128] = jnp.where(hit, 1.0, 0.0).astype(BF)
        left = ds_ref[:, 16 * g : 16 * g + 16, :].reshape(heads * 16, queries)
        acc[...] += dot(left, table[...], NT)

    @pl.when(step == pl.num_programs(0) - 1)
    def _():
        row = lax.broadcasted_iota(jnp.int32, acc.shape, 0) % 16
        col = lax.broadcasted_iota(jnp.int32, acc.shape, 1) // 32
        out_ref[...] = jnp.where(row == col, acc[...], 0.0)


def bucket_sums(place, half, buckets_t, ds):
    heads, keys, queries = ds.shape
    per = keys // 128

    def source(j, place):
        return ((place[1] ^ half) * per + (place[0] ^ j), 0)

    full = call(
        bucket_kernel,
        sds((heads * 16, 512), F32),
        "bucket_sums",
        grid=(per,),
        in_specs=[pl.BlockSpec((128, queries), source), pl.BlockSpec((heads, 128, queries), lambda j, p: (0, j, 0))],
        out_specs=whole(heads * 16, 512),
        scratch=[pltpu.VMEM((heads * 16, 512), F32), pltpu.VMEM((512, queries), BF)],
        prefetch=1,
    )(place, buckets_t, ds)
    return jnp.sum(full.reshape(heads, 16, 16, 32), axis=(1, 2))


def move(value, move_to, sizes):
    shards, ctx, tps = sizes
    pairs = []
    for s in range(shards):
        for c in range(ctx):
            for t in range(tps):
                a, b, d = move_to(s, c, t)
                pairs.append(((s * ctx + c) * tps + t, (a * ctx + b) * tps + d))
    return lax.ppermute(value, ALL, pairs)


def body(
    hidden_in,
    norm_attn_gain,
    query_weight,
    key_weight,
    value_weight,
    out_weight,
    bias_table,
    norm_ffn_gain,
    ffn_in_weight,
    ffn_out_weight,
    buckets,
    output_gradient,
):
    sizes = tuple(lax.axis_size(a) for a in ALL)
    shards, ctxs, tps = sizes
    s, c, t = (lax.axis_index(a) for a in ALL)
    fast = shards == 4
    assert ctxs == 2 and tps == 4 and hidden_in.shape[0] == tps
    heads = bias_table.shape[1]

    def along(k):
        return lambda a, b, d: (a, b, d ^ k)

    def across(a, b, d):
        return (a, 1 - b, d)

    def near(a, b, d):
        return (a ^ (1 if b == 0 else 2), b, d)

    def far(a, b, d):
        return (a ^ (2 if b == 0 else 1), b, d)

    go = partial(move, sizes=sizes)

    def spot(shard, core):
        d = shard ^ s
        return jnp.where(core == 0, d, (d >> 1) | ((d & 1) << 1)) if fast else jnp.int32(shard)

    place = jnp.stack(
        [t, c] + [spot(i, c) for i in range(4)] + [spot(i, 1 - c) for i in range(4)]
    ).astype(jnp.int32)

    def exchange_rows(value):
        picked = [lax.dynamic_index_in_dim(value, t ^ k, 0, keepdims=False) for k in range(tps)]
        return [picked[0]] + [go(picked[k], along(k)) for k in range(1, tps)]

    def gather(half):
        blocks = jnp.stack([half] + [go(half, along(k)) for k in range(1, tps)])
        if fast:
            pair = jnp.stack([blocks, go(blocks, near)])
            full = jnp.concatenate([pair, go(pair, far)])
        else:
            full = lax.all_gather(blocks, "shard", axis=0, tiled=False)
            full = jnp.swapaxes(full, 0, 1).reshape(tps, 4, 192, 384).swapaxes(0, 1)
        return full, go(full, across)

    def scatter(keep, send):
        def add(a, b):
            return (a.astype(F32) + b.astype(F32)).astype(BF)

        total = add(keep, go(send, across))
        if fast:
            total = add(total[:2], go(total[2:], far))
            total = add(total[0], go(total[1], near))
        else:
            rows = 4 * 192 // shards
            total = total.swapaxes(0, 1).reshape(tps, shards, rows, 384).swapaxes(0, 1)
            total = lax.psum_scatter(total, "shard", scatter_dimension=0, tiled=False)
        got = [total[0]] + [go(total[k], along(k)) for k in range(1, tps)]
        got = [v.astype(F32) for v in got]
        mine = ((got[0] + got[1]) + (got[2] + got[3])).astype(BF)
        other = go(mine, across)
        lo = jnp.where(c == 0, mine, other)
        hi = jnp.where(c == 0, other, mine)
        return lo.astype(F32), hi.astype(F32)

    rows = query_weight.shape[0]
    out_rows = out_weight.shape[0]
    out_pack = jnp.concatenate([out_weight[:, 192 * i : 192 * i + 192] for i in range(4)], axis=0)

    def my_half(lo, hi):
        return jnp.where(c == 0, lo, hi)

    att_half = my_half(
        jnp.concatenate([query_weight, key_weight], axis=1), jnp.concatenate([value_weight, out_pack], axis=1)
    )
    w1_half = my_half(ffn_in_weight[:, :384], ffn_in_weight[:, 384:])
    w2_half = my_half(ffn_out_weight[:, :384], ffn_out_weight[:, 384:])
    x_parts = exchange_rows(hidden_in)
    am, ao = gather(att_half)
    g_parts = exchange_rows(output_gradient)
    w1m, w1o = gather(w1_half)
    w2m, w2o = gather(w2_half)
    if not fast:
        def regroup(z):
            part = z[..., 192:].reshape(4, 4, shards // 4, 4, out_rows, 192)
            part = jnp.transpose(part, (0, 1, 3, 2, 4, 5)).reshape(4, 4, 192, 192)
            return jnp.concatenate([z[..., :192], part], axis=-1)

        fixed_m, fixed_o = regroup(am), regroup(ao)
        am, ao = jnp.where(c == 1, fixed_m, am), jnp.where(c == 0, fixed_o, ao)

    head_order = jnp.concatenate([(t ^ k) * (heads // tps) + jnp.arange(heads // tps) for k in range(tps)])
    table_rel = jnp.pad(jnp.take(bias_table.T, head_order, axis=0), ((0, 0), (0, 128 - bias_table.shape[0])))
    buckets_t = buckets.T
    bias = position_bias(place, table_rel, buckets_t)

    width = hidden_in.shape[2]
    n = 512
    ga = norm_attn_gain.reshape(1, width)
    gf = norm_ffn_gain.reshape(1, width)
    row = sds((n, width), BF)
    x, xn, q, k, v, a_full, o_full = call(
        qkv_kernel,
        (row, row, row, row, row, sds((4, width, width), BF), sds((width, width), BF)),
        "qkv",
        prefetch=1,
        in_specs=[whole(128, width)] * 4 + [whole(1, width), whole(4, 4, 192, 384), whole(4, 4, 192, 384)],
        out_specs=(whole(n, width),) * 5 + (whole(4, width, width), whole(width, width)),
    )(place, *x_parts, ga, am, ao)
    k_other, v_other = go(k, across), go(v, across)
    att, att_full, lse = attend(q, k, v, k_other, v_other, bias)
    mid, nf = call(
        project_kernel,
        (sds((n, width), F32), row),
        "project",
        in_specs=[whole(n, width), whole(n, width), whole(width, width), whole(1, width)],
        out_specs=(whole(n, width), whole(n, width)),
    )(x, att, o_full, gf)

    carry = None
    grads = []
    for kk in range(4):
        out_acc, dnf, *g4 = ffn_block(kk, place, nf, g_parts, w1m, w1o, w2m, w2o, carry)
        carry = (out_acc, dnf)
        grads.append(g4)
    keep1, keep2, send1, send2 = (jnp.stack([g[i] for g in grads], axis=1) for i in range(4))
    w1_grad = scatter(keep1, send1)
    w2_grad = scatter(keep2, send2)

    hid, dmid, dml, da, delta, gf_grad = call(
        turn_kernel,
        (row, sds((n, width), F32), row, row, sds((heads, n), F32), sds((1, width), F32)),
        "turn",
        in_specs=[whole(n, width)] * 3 + [whole(128, width)] * 4 + [whole(1, width), whole(width, width), whole(n, width)],
        out_specs=(whole(n, width),) * 4 + (whole(heads, n), whole(1, width)),
    )(mid, out_acc, dnf, *g_parts, gf, o_full, att_full)
    delta = delta.reshape(heads // 2, 2, n)

    def return_rows(value):
        pieces = [value[0:128]] + [go(value[128 * k : 128 * k + 128], along(k)) for k in range(1, tps)]
        stacked = jnp.stack(pieces)
        return jnp.stack([lax.dynamic_index_in_dim(stacked, t ^ i, 0, keepdims=False) for i in range(tps)])

    hidden_out = return_rows(hid)

    dq_part, dk_send, dv_send, ds1 = attend_back(1, q, da, k_other, v_other, bias, lse, delta, None)
    dk_add, dv_add = go(dk_send, across), go(dv_send, across)
    dq, dk, dv, ds0 = attend_back(0, q, da, k, v, bias, lse, delta, dq_part)
    keep_a, send_a, back, ga_grad = call(
        weights_kernel,
        (sds((4, 4, 192, 384), BF), sds((4, 4, 192, 384), BF), row, sds((1, width), F32)),
        "weights",
        prefetch=1,
        in_specs=[whole(n, width)] * 6
        + [whole(4, width, width)]
        + [whole(n, width)] * 4
        + [whole(1, width)],
        out_specs=(whole(4, 4, 192, 384), whole(4, 4, 192, 384), whole(n, width), whole(1, width)),
    )(place, xn, dq, dk, dv, dk_add, dv_add, a_full, att, dml, dmid, x, ga)
    if not fast:
        def ungroup(z):
            part = z[..., 192:].reshape(4, 4, 4, shards // 4, out_rows, 192)
            part = jnp.transpose(part, (0, 1, 3, 2, 4, 5)).reshape(4, 4, 192, 192)
            return jnp.concatenate([z[..., :192], part], axis=-1)

        keep_a, send_a = (
            jnp.where(c == 1, ungroup(keep_a), keep_a),
            jnp.where(c == 0, ungroup(send_a), send_a),
        )
    hidden_grad = return_rows(back).astype(F32)
    att_lo, att_hi = scatter(keep_a, send_a)
    table_sum = bucket_sums(place, 1, buckets_t, ds1) + bucket_sums(place, 0, buckets_t, ds0)
    table_abs = jnp.zeros((heads, bias_table.shape[0]), F32).at[head_order].set(table_sum)

    small = jnp.concatenate([ga_grad.reshape(-1), gf_grad.reshape(-1), table_abs.reshape(-1)])
    small = jnp.pad(small, (0, 2048 - small.shape[0])).reshape(16, 128)
    small = small + go(small, across)
    s1, s2, s3 = (go(small, along(k)) for k in (1, 2, 3))
    small = (small + s1) + (s2 + s3)
    if fast:
        s1, s2, s3 = (go(small, lambda a, b, d, k=k: (a ^ k, b, d)) for k in (1, 2, 3))
        small = (small + s1) + (s2 + s3)
    else:
        small = lax.psum(small, "shard")
    small = small.reshape(-1)
    table_grad = small[2 * width : 2 * width + table_abs.size].reshape(table_abs.shape).T

    out_grad = jnp.concatenate([att_hi[out_rows * i : out_rows * i + out_rows, 192:] for i in range(4)], axis=1)
    return (
        hidden_out,
        hidden_grad,
        small[:width],
        att_lo[:, :192],
        att_lo[:, 192:],
        att_hi[:, :192],
        out_grad,
        table_grad,
        small[width : 2 * width],
        jnp.concatenate(w1_grad, axis=1),
        jnp.concatenate(w2_grad, axis=1),
    )


def solution(mesh):
    rows = P("shard", ("ctx", "tp"), None)
    cols = P("shard", "tp")
    both = P(("tp", "shard"), None)
    return jax.shard_map(
        body,
        mesh=mesh,
        in_specs=(rows, P(), cols, cols, cols, both, P(), P(), cols, both, P("ctx", None), rows),
        out_specs=(rows, rows, P(), cols, cols, cols, both, P(), P(), cols, both),
        check_vma=False,
    )
```

```python
from functools import partial

import jax
import jax.numpy as jnp
from jax import lax
from jax.experimental import pallas as pl
from jax.experimental.pallas import tpu as pltpu
from jax.sharding import PartitionSpec as P

EPS = 1e-06
F32 = jnp.float32
BF = jnp.bfloat16
ALL = ("shard", "ctx", "tp")
NN = (((1,), (0,)), ((), ()))
NT = (((1,), (1,)), ((), ()))
TN = (((0,), (0,)), ((), ()))


def dot(a, b, dims=NN):
    return lax.dot_general(a, b, dims, preferred_element_type=F32)


COST = {
    "fence": (60, 1),
    "position_bias": (60, 12),
    "qkv": (60, 16),
    "attend": (60, 24),
    "project": (60, 12),
    "ffn": (60, 32),
    "turn": (60, 16),
    "attend_back": (60, 24),
    "bucket_sums": (60, 16),
    "weights": (60, 24),
}


def call(kernel, args, out_shape, name, in_specs, out_specs, grid=(), scratch=(), deps=(), aliases=None):
    inputs = len(in_specs)
    outputs = inputs + len(deps) + len(out_shape)
    any_space = pl.BlockSpec(memory_space=pl.ANY)

    def wrapped(*refs):
        kernel(*refs[:inputs], *refs[inputs + len(deps) : outputs], *refs[outputs + 1 :])

    cost, room = COST[name]
    return pl.pallas_call(
        wrapped,
        out_shape=[*out_shape, sds((8, 128), F32)],
        grid=grid,
        in_specs=[*in_specs] + [any_space] * len(deps),
        out_specs=[*out_specs, any_space],
        scratch_shapes=scratch,
        compiler_params=pltpu.CompilerParams(vmem_limit_bytes=room * 1024 * 1024),
        input_output_aliases=aliases or {},
        cost_estimate=pl.CostEstimate(
            flops=cost * 1000000000, transcendentals=0, bytes_accessed=cost * 2000000
        ),
        name=name,
    )(*args, *deps)


def fence(*deps):
    return call(lambda: None, (), [], "fence", [], [], deps=jax.tree.leaves(deps))[0]


def in_hbm(value):
    return pltpu.with_memory_space_constraint(value, pltpu.HBM)


VM = pl.BlockSpec(memory_space=pltpu.VMEM)
SM = pl.BlockSpec(memory_space=pltpu.SMEM)


def whole(*shape):
    return pl.BlockSpec(shape, lambda *_: (0,) * len(shape))


def sds(shape, dtype):
    return jax.ShapeDtypeStruct(shape, dtype)


def bias_kernel(half, place, table_ref, buckets_ref, out_ref):
    tp = place[0]
    heads = table_ref.shape[0]
    keys, queries = buckets_ref.shape
    per = keys // 256
    step = pl.program_id(0)
    block = (place[1] ^ half) * per + (tp ^ step)
    first = pl.multiple_of(block * 128, 128)
    for k in range(queries // 128):
        start = pl.multiple_of((tp ^ k) * 128, 128)
        index = buckets_ref[pl.ds(first, 128), pl.ds(start, 128)]
        for h in range(heads):
            row = jnp.broadcast_to(table_ref[h : h + 1, :], index.shape)
            out_ref[h, :, 128 * k : 128 * k + 128] = jnp.take_along_axis(
                row, index, axis=1, mode="promise_in_bounds"
            ).astype(BF)


def position_bias(place, table_rel, buckets_t, half, deps):
    heads = table_rel.shape[0]
    keys, queries = buckets_t.shape
    return call(
        partial(bias_kernel, half),
        (place, table_rel, buckets_t),
        [pltpu.HBM((heads, keys // 2, queries), BF)],
        "position_bias",
        [SM, VM, VM],
        [pl.BlockSpec((heads, 128, queries), lambda j: (0, j, 0))],
        grid=(keys // 256,),
        deps=deps,
    )


def qkv_kernel(place, x0, x1, x2, x3, gain, mine, other, x_out, xn_out, q_out, kv_out, a_out, o_out):
    first = place[1] == 0
    for r, ref in enumerate((x0, x1, x2, x3)):
        x = ref[...]
        x_out[128 * r : 128 * r + 128, :] = x
        xf = x.astype(F32)
        scale = lax.rsqrt(jnp.mean(xf * xf, axis=-1, keepdims=True) + EPS)
        xn_out[128 * r : 128 * r + 128, :] = (xf * scale * gain[...]).astype(BF)
    for k in range(4):
        for s in range(4):
            m = mine[place[2 + s], k]
            o = other[place[6 + s], k]
            a_out[k, 192 * s : 192 * s + 192, 0:384] = jnp.where(first, m, o)
            a_out[k, 192 * s : 192 * s + 192, 384:768] = jnp.where(first, o, m)
        for s in range(4):
            for c in range(4):
                o_out[192 * k + 48 * s : 192 * k + 48 * s + 48, 192 * c : 192 * c + 192] = a_out[
                    k, 192 * s + 48 * c : 192 * s + 48 * c + 48, 576:768
                ]
        y = dot(xn_out[...], a_out[k, :, 0:576]).astype(BF)
        q_out[:, 192 * k : 192 * k + 192] = y[:, 0:192]
        kv_out[0, :, 192 * k : 192 * k + 192] = y[:, 192:384]
        kv_out[1, :, 192 * k : 192 * k + 192] = y[:, 384:576]


def attend_kernel(q_ref, k0_ref, v0_ref, k1_ref, v1_ref, bias0, bias1, *refs):
    att_ref, full_ref, lse_ref = refs[-3:]
    part_keys = k0_ref.shape[0] // 2
    rows = q_ref.shape[0]
    qt = q_ref[...].T
    vts = [v0_ref[...].T, v1_ref[...].T]
    side = lax.broadcasted_iota(jnp.int32, qt.shape, 0) // 64
    ones = jnp.ones((16, part_keys), BF)
    results = []
    for h in range(2):
        q = jnp.where(side == h, qt, jnp.zeros((), BF))
        scores = []
        top = None
        for i in range(4):
            keys = (k0_ref, k1_ref)[i // 2][part_keys * (i % 2) : part_keys * (i % 2 + 1), :]
            bias = (bias0, bias1)[i // 2][h, part_keys * (i % 2) : part_keys * (i % 2 + 1), :]
            score = dot(keys, q) + bias.astype(F32)
            high = jnp.max(score, axis=0, keepdims=True)
            top = high if i == 0 else jnp.maximum(top, high)
            scores.append(score)
        part = None
        for i, score in enumerate(scores):
            values = vts[i // 2][64 * h : 64 * h + 64, part_keys * (i % 2) : part_keys * (i % 2 + 1)]
            e = jnp.exp(score - top).astype(BF)
            piece = dot(jnp.concatenate([values, ones], axis=0), e)
            part = piece if i == 0 else part + piece
        total = part[64:65, :]
        lse_ref[0, h : h + 1, :] = top + jnp.log(total)
        results.append(part[0:64, :] / total)
    full = jnp.concatenate(results, axis=0).T
    full_ref[...] = full
    att_ref[...] = full.astype(BF)


def attend(q, own, other, bias, begin, pairs, before, deps):
    rows, width = q.shape
    keys = own.shape[1]
    col = pl.BlockSpec((rows, 128), lambda p: (0, p + begin))
    kv = [pl.BlockSpec((None, rows, 128), lambda p, i=i: (i, 0, p + begin)) for i in range(2)]
    return call(
        attend_kernel,
        (q, own, own, other, other, in_hbm(bias[0]), in_hbm(bias[1]), *before),
        [sds((rows, width), BF), sds((rows, width), F32), sds((width // 128, 2, rows), F32)],
        "attend",
        [col] + kv * 2 + [pl.BlockSpec((2, keys, rows), lambda p: (p + begin, 0, 0))] * 2
        + [pl.BlockSpec(memory_space=pl.ANY)] * len(before),
        [col, col, pl.BlockSpec((1, 2, rows), lambda p: (p + begin, 0, 0))],
        grid=(pairs,),
        deps=deps,
        aliases={7: 0, 8: 1, 9: 2} if before else None,
    )


def project_kernel(x_ref, att_ref, o_ref, gain, mid_ref, nf_ref):
    mid = x_ref[...].astype(F32) + dot(att_ref[...], o_ref[...])
    mid_ref[...] = mid
    scale = lax.rsqrt(jnp.mean(mid * mid, axis=-1, keepdims=True) + EPS)
    nf_ref[...] = (mid * scale * gain[...]).astype(BF)


def ffn_kernel(first_call, place, nf_ref, g0, g1, g2, g3, mine, other, *refs):
    if first_call:
        out_ref, dnf_ref, keep, send, w1s, w2s, gs, us, ds = refs
    else:
        out_in, dnf_in = refs[:2]
        out_ref, dnf_ref, keep, send, w1s, w2s, gs, us, ds = refs[-9:]
    first = place[1] == 0
    step = pl.program_id(0)

    @pl.when(step == 0)
    def _():
        for r, ref in enumerate((g0, g1, g2, g3)):
            gs[128 * r : 128 * r + 128, :] = ref[...]
        if first_call:
            out_ref[...] = jnp.zeros_like(out_ref)
            dnf_ref[...] = jnp.zeros_like(dnf_ref)
        else:
            out_ref[...] = out_in[...]
            dnf_ref[...] = dnf_in[...]

    for s in range(4):
        rows = slice(192 * s, 192 * s + 192)
        for i, w in enumerate((w1s, w2s)):
            m = mine[place[2 + s], 0, i]
            o = other[place[6 + s], 0, i]
            w[rows, 0:384] = jnp.where(first, m, o)
            w[rows, 384:768] = jnp.where(first, o, m)
    for j in range(3):
        cols = slice(256 * j, 256 * j + 256)
        v = dot(nf_ref[...], w1s[:, cols])
        square = v * v
        th = jnp.tanh(v * (0.7978845608 + (0.7978845608 * 0.044715) * square))
        half = 0.5 + 0.5 * th
        us[:, cols] = (v * half).astype(BF)
        slope = half + v * (0.5 - 0.5 * th * th) * (0.7978845608 + (0.7978845608 * 3 * 0.044715) * square)
        ds[:, cols] = (dot(gs[...], w2s[cols, :], NT) * slope).astype(BF)
    out_ref[...] += dot(us[...], w2s[...])
    dnf_ref[...] += dot(ds[...], w1s[...], NT)
    d1 = dot(nf_ref[...], ds[...], TN).astype(BF)
    d2 = dot(us[...], gs[...], TN).astype(BF)
    for s in range(4):
        rows = slice(192 * s, 192 * s + 192)
        for i, d in enumerate((d1, d2)):
            lo = d[rows, 0:384]
            hi = d[rows, 384:768]
            keep[place[2 + s], 0, i] = jnp.where(first, lo, hi)
            send[place[6 + s], 0, i] = jnp.where(first, hi, lo)


def ffn_blocks(place, nf, g, mine, other, carry, grads, begin, count, deps):
    rows, width = nf.shape
    spec = pl.BlockSpec((4, 1, 2, 192, 384), lambda i: (0, i + begin, 0, 0, 0))
    aliases = {}
    if carry:
        aliases = {8: 0, 9: 1}
    if grads:
        aliases.update({10: 2, 11: 3})
    return call(
        partial(ffn_kernel, not carry),
        (place, nf, *g, mine, other, *carry, *grads),
        [sds((rows, width), F32), sds((rows, width), F32)] + [sds(mine.shape, BF)] * 2,
        "ffn",
        [SM] + [VM] * 5 + [spec] * 2 + [VM] * len(carry) + [pl.BlockSpec(memory_space=pl.ANY)] * len(grads),
        [VM, VM, spec, spec],
        grid=(count,),
        scratch=[pltpu.VMEM((width, width), BF)] * 2 + [pltpu.VMEM((rows, width), BF)] * 3,
        deps=deps,
        aliases=aliases,
    )


def turn_kernel(mid_ref, out_in, dnf_in, g0, g1, g2, g3, gain, o_ref, full_ref, hid_ref, dmid_ref, dml_ref, da_ref, delta_ref, gg_ref):
    mid = mid_ref[...]
    hid_ref[...] = (mid + out_in[...]).astype(BF)
    scale = lax.rsqrt(jnp.mean(mid * mid, axis=-1, keepdims=True) + EPS)
    up = dnf_in[...]
    weighted = up * gain[...]
    mean_term = jnp.mean(weighted * mid, axis=-1, keepdims=True)
    res = scale * weighted - mid * (scale * scale * scale) * mean_term
    gg_ref[...] = jnp.sum(up * mid * scale, axis=0, keepdims=True)
    for r, ref in enumerate((g0, g1, g2, g3)):
        rows = slice(128 * r, 128 * r + 128)
        dmid_ref[rows, :] = res[rows, :] + ref[...].astype(F32)
    low = dmid_ref[...].astype(BF)
    dml_ref[...] = low
    da = dot(low, o_ref[...], NT).astype(BF)
    da_ref[...] = da
    pairs = delta_ref.shape[0]
    width = da.shape[1]
    head = lax.broadcasted_iota(jnp.int32, (2 * pairs, width), 0)
    lane = lax.broadcasted_iota(jnp.int32, (2 * pairs, width), 1)
    pick = jnp.where(lane // 64 == head, 1.0, 0.0)
    delta = lax.dot_general(
        pick, da.astype(F32) * full_ref[...], NT, precision=lax.Precision.HIGHEST, preferred_element_type=F32
    )
    for p in range(pairs):
        delta_ref[p] = delta[2 * p : 2 * p + 2, :]


def split_rows(value, other):
    row = lax.broadcasted_iota(jnp.int32, (64, value.shape[1]), 0)
    out = jnp.zeros((64, value.shape[1]), BF)
    for i in range(3):
        piece = value.astype(BF)
        out = jnp.where(row == i, piece, out)
        value = value - piece.astype(F32)
    return out


def attend_back_kernel(last, q_ref, da_ref, k_ref, v_ref, bias_ref, lse_ref, delta_ref, *refs):
    if last:
        dq_in, dq_ref, dkv_ref, ds_ref = refs
    else:
        dq_ref, dkv_ref, ds_ref = refs
    part_keys = k_ref.shape[0] // 2
    zero = jnp.zeros((), BF)
    qt = q_ref[...].T
    dat = da_ref[...].T
    kt = k_ref[...].T
    lane = lax.broadcasted_iota(jnp.int32, (1, 128), 1)
    dqs = [None, None]
    qs, das, qas, daas = [], [], [], []
    for h in range(2):
        own = lane // 64 == h
        qs.append(jnp.where(own, q_ref[...], zero))
        das.append(jnp.where(own, da_ref[...], zero))
        for t, stat, out in ((qt, lse_ref, qas), (dat, delta_ref, daas)):
            extra = split_rows(stat[0, h : h + 1, :], None)
            mine = t[64 * h : 64 * h + 64, :]
            out.append(jnp.concatenate([mine, extra] if h == 0 else [extra, mine], axis=0))
    for i in range(2):
        rows = slice(part_keys * i, part_keys * (i + 1))
        k = k_ref[rows, :]
        v = v_ref[rows, :]
        dk = dv = None
        for h in range(2):
            own = lane // 64 == h
            minus = jnp.where(lane % 64 < 3, -1.0, 0.0).astype(BF)
            p = jnp.exp(dot(jnp.where(own, k, minus), qas[h]) + bias_ref[h, rows, :].astype(F32))
            ds = (p * dot(jnp.where(own, v, minus), daas[h])).astype(BF)
            ds_ref[h, rows, :] = ds
            a = dot(kt[64 * h : 64 * h + 64, rows], ds)
            b = dot(ds, qs[h])
            c = dot(p.astype(BF), das[h])
            dqs[h] = a if i == 0 else dqs[h] + a
            dk, dv = (b, c) if h == 0 else (dk + b, dv + c)
        dkv_ref[0, rows, :] = dk.astype(dkv_ref.dtype)
        dkv_ref[1, rows, :] = dv.astype(dkv_ref.dtype)
    dq = jnp.concatenate(dqs, axis=0).T
    if last:
        dq_ref[...] = (dq_in[...] + dq).astype(dq_ref.dtype)
    else:
        dq_ref[...] = dq


def attend_back(q, da, kv, bias, begin, pairs, lse, delta, dq, deps):
    rows = q.shape[0]
    width = 128 * pairs
    keys = kv.shape[1]
    col = pl.BlockSpec((rows, 128), lambda p: (0, p + begin))
    out = pl.BlockSpec((rows, 128), lambda p: (0, p))
    stat = pl.BlockSpec((1, 2, rows), lambda p: (p + begin, 0, 0))
    each = [pl.BlockSpec((None, keys, 128), lambda p, i=i: (i, 0, p + begin)) for i in range(2)]
    last = len(dq) > 0
    return call(
        partial(attend_back_kernel, last),
        (q, da, kv, kv, in_hbm(bias), lse, delta, *dq),
        [
            sds((rows, width), BF if last else F32),
            sds((2, keys, width), F32 if last else BF),
            pltpu.HBM((2 * pairs, keys, rows), BF),
        ],
        "attend_back",
        [col] * 2 + each + [pl.BlockSpec((2, keys, rows), lambda p: (p + begin, 0, 0)), stat, stat] + [out] * len(dq),
        [
            out,
            pl.BlockSpec((2, keys, 128), lambda p: (0, 0, p)),
            pl.BlockSpec((2, keys, rows), lambda p: (p, 0, 0)),
        ],
        grid=(pairs,),
        deps=deps,
    )


def weights_kernel(blocks, last, place, xn_ref, dq_ref, dkv_in, dkv_add, a_ref, att_ref, dml_ref, *refs):
    if last:
        up_in, dmid_ref, x_ref, gain, keep, send, back_ref, gg_ref = refs
        up = up_in[...]
    else:
        keep, send, up_ref = refs
        up = None
    first = place[1] == 0
    dq = dq_ref[...]
    dk, dv = ((dkv_in[i] + dkv_add[i].astype(F32)).astype(BF) for i in range(2))
    xn = xn_ref[...]
    for i, k in enumerate(blocks):
        cols = slice(192 * i, 192 * i + 192)
        cat = jnp.concatenate([dq[:, cols], dk[:, cols], dv[:, cols]], axis=1)
        part = dot(cat, a_ref[k, :, 0:576], NT)
        up = part if up is None else up + part
        grad = dot(xn, cat, TN).astype(BF)
        out = dot(att_ref[:, 192 * k : 192 * k + 192], dml_ref[...], TN).astype(BF)
        for s in range(4):
            rows = slice(192 * s, 192 * s + 192)
            lo = grad[rows, 0:384]
            piece = jnp.concatenate(
                [out[48 * s : 48 * s + 48, 192 * c : 192 * c + 192] for c in range(4)], axis=0
            )
            hi = jnp.concatenate([grad[rows, 384:576], piece], axis=1)
            keep[place[2 + s], i] = jnp.where(first, lo, hi)
            send[place[6 + s], i] = jnp.where(first, hi, lo)
    if not last:
        up_ref[...] = up
        return
    x = x_ref[...].astype(F32)
    scale = lax.rsqrt(jnp.mean(x * x, axis=-1, keepdims=True) + EPS)
    weighted = up * gain[...]
    mean_term = jnp.mean(weighted * x, axis=-1, keepdims=True)
    res = scale * weighted - x * (scale * scale * scale) * mean_term
    gg_ref[...] = jnp.sum(up * x * scale, axis=0, keepdims=True)
    back_ref[...] = (dmid_ref[...] + res).astype(BF)


def bucket_kernel(source, place, buckets_ref, ds0_ref, ds1_ref, out_ref, acc, table):
    tp = place[0]
    step = pl.program_id(0)
    heads, group, queries = ds0_ref.shape
    blocks = queries // 128
    first = ((place[1] ^ source) * (buckets_ref.shape[0] // 256) + (tp ^ step)) * 128

    @pl.when(step == 0)
    def _():
        acc[...] = jnp.zeros_like(acc)

    label = [(lax.broadcasted_iota(jnp.int32, (16, 128), 0) + 16 * i).astype(F32).astype(BF) for i in range(2)]
    one, zero = jnp.ones((), BF), jnp.zeros((), BF)
    for g in range(group // 16):
        for k in range(blocks):
            start = pl.multiple_of((tp ^ k) * 128, 128)
            index = buckets_ref[pl.ds(pl.multiple_of(first + 16 * g, 16), 16), pl.ds(start, 128)].astype(F32)
            for j in range(16):
                spread = jnp.broadcast_to(index[j : j + 1, :], (16, 128)).astype(BF)
                for i in range(2):
                    at = 32 * j + 16 * i
                    table[at : at + 16, 128 * k : 128 * k + 128] = jnp.where(spread == label[i], one, zero)
        left = [d[:, 16 * g : 16 * g + 16, :].reshape(heads * 16, queries) for d in (ds0_ref, ds1_ref)]
        acc[...] += dot(jnp.concatenate(left, axis=0), table[...], NT)

    @pl.when(step == pl.num_programs(0) - 1)
    def _():
        row = lax.broadcasted_iota(jnp.int32, acc.shape, 0) % 16
        col = lax.broadcasted_iota(jnp.int32, acc.shape, 1) // 32
        out_ref[...] = jnp.where(row == col, acc[...], 0.0)


def bucket_sums(place, half, buckets_t, ds, deps):
    heads, keys, queries = ds[0].shape
    spec = pl.BlockSpec((heads, 128, queries), lambda j: (0, j, 0))
    return call(
        partial(bucket_kernel, half),
        (place, buckets_t, in_hbm(ds[0]), in_hbm(ds[1])),
        [sds((heads * 32, 512), F32)],
        "bucket_sums",
        [SM, VM, spec, spec],
        [whole(heads * 32, 512)],
        grid=(keys // 128,),
        scratch=[pltpu.VMEM((heads * 32, 512), F32), pltpu.VMEM((512, queries), BF)],
        deps=deps,
    )


def move(value, move_to, sizes):
    shards, ctx, tps = sizes
    pairs = []
    for s in range(shards):
        for c in range(ctx):
            for t in range(tps):
                a, b, d = move_to(s, c, t)
                pairs.append(((s * ctx + c) * tps + t, (a * ctx + b) * tps + d))
    return lax.ppermute(value, ALL, pairs)


def body(
    hidden_in,
    norm_attn_gain,
    query_weight,
    key_weight,
    value_weight,
    out_weight,
    bias_table,
    norm_ffn_gain,
    ffn_in_weight,
    ffn_out_weight,
    buckets,
    output_gradient,
):
    sizes = tuple(lax.axis_size(a) for a in ALL)
    shards, ctxs, tps = sizes
    s, c, t = (lax.axis_index(a) for a in ALL)
    fast = shards == 4
    assert ctxs == 2 and tps == 4 and hidden_in.shape[0] == tps
    heads = bias_table.shape[1]

    def along(k):
        return lambda a, b, d: (a, b, d ^ k)

    def across(a, b, d):
        return (a, 1 - b, d)

    def near(a, b, d):
        return (a ^ (1 if b == 0 else 2), b, d)

    def far(a, b, d):
        return (a ^ (2 if b == 0 else 1), b, d)

    go = partial(move, sizes=sizes)

    def spot(shard, core):
        d = shard ^ s
        return jnp.where(core == 0, d, (d >> 1) | ((d & 1) << 1)) if fast else jnp.int32(shard)

    place = jnp.stack(
        [t, c] + [spot(i, c) for i in range(4)] + [spot(i, 1 - c) for i in range(4)]
    ).astype(jnp.int32)

    def pick(value, k):
        return lax.dynamic_index_in_dim(value, t ^ k, 0, keepdims=False)

    def tie(value, token):
        return lax.optimization_barrier((value, token))

    def add(a, b):
        return (a.astype(F32) + b.astype(F32)).astype(BF)

    def send_near(value):
        return go(value, near) if fast else value

    def send_far(value):
        return go(value, far) if fast else value

    def join_near(value, got):
        return jnp.stack([value, got]) if fast else value

    def join_far(value, got):
        if fast:
            return jnp.concatenate([value, got])
        full = lax.all_gather(value, "shard", axis=0, tiled=False)
        full = jnp.moveaxis(full, 0, -3)
        lead = full.shape[:-3]
        return jnp.moveaxis(full.reshape(lead + (4, 192, 384)), -3, 0)

    def stage_far(keep, got):
        if fast:
            return add(keep[:2], got[:2]), add(keep[2:], got[2:])
        return add(keep, got), jnp.zeros((8, 128), BF)

    def stage_near(stay, got):
        return (add(stay[0], got[0]), add(stay[1], got[1])) if fast else (stay, got)

    def stage_last(stay, got):
        if fast:
            return [add(stay[i], got[i]) for i in range(stay.shape[0])]
        total = jnp.moveaxis(stay, 0, -3)
        lead = total.shape[:-3]
        total = jnp.moveaxis(total.reshape(lead + (shards, 768 // shards, 384)), -3, 0)
        total = lax.psum_scatter(total, "shard", scatter_dimension=0, tiled=False)
        return [total[i] for i in range(total.shape[0])]

    def my_half(lo, hi):
        return jnp.where(c == 0, lo, hi)

    def both_halves(mine, other):
        return jnp.where(c == 0, mine, other).astype(F32), jnp.where(c == 0, other, mine).astype(F32)

    width = hidden_in.shape[2]
    n = 512
    ga = norm_attn_gain.reshape(1, width)
    gf = norm_ffn_gain.reshape(1, width)
    row = sds((n, width), BF)
    out_rows = out_weight.shape[0]

    out_pack = jnp.concatenate([out_weight[:, 192 * i : 192 * i + 192] for i in range(4)], axis=0)
    att_half = my_half(
        jnp.concatenate([query_weight, key_weight], axis=1), jnp.concatenate([value_weight, out_pack], axis=1)
    )
    ffn_half = my_half(
        jnp.stack([ffn_in_weight[:, :384], ffn_out_weight[:, :384]]),
        jnp.stack([ffn_in_weight[:, 384:], ffn_out_weight[:, 384:]]),
    )
    head_order = jnp.concatenate([(t ^ k) * (heads // tps) + jnp.arange(heads // tps) for k in range(tps)])
    table_rel = jnp.pad(jnp.take(bias_table.T, head_order, axis=0), ((0, 0), (0, 128 - bias_table.shape[0])))
    buckets_t = buckets.T

    def both(value, token):
        return lax.optimization_barrier((value, token))

    za = [go(att_half, along(k)) for k in (1, 2, 3)]
    xs = [pick(hidden_in, k) for k in range(tps)]
    a0 = jnp.stack([att_half] + za)
    (ffn_w, xs), a0 = both((ffn_half, xs), a0)
    a1 = send_near(a0)
    zw2, zw3 = (go(ffn_w, along(k)) for k in (2, 3))
    bias = [None] * 2
    bias[0], tok = position_bias(place, table_rel, buckets_t, 0, [a0, ffn_w, *xs])
    a1, tok = tie(a1, tok)
    a1 = join_near(a0, a1)
    am = send_far(a1)
    bias[1], tok = position_bias(place, table_rel, buckets_t, 1, [tok, a1])
    (zw2, zw3), tok = tie((zw2, zw3), tok)
    p1 = jnp.stack([zw2, zw3])
    xs, p1 = both(xs, p1)
    zx = [go(xs[k], along(k)) for k in (1, 2, 3)]
    p1n = send_near(p1)
    tok = fence(tok, xs, p1)
    am, tok = tie(am, tok)
    am = join_far(a1, am)
    ao = go(am, across)
    tok = fence(tok, am)
    p1n, tok = tie(p1n, tok)
    p1 = join_near(p1, p1n)
    p1m = send_far(p1)
    tok = fence(tok, p1)
    zx, tok = tie(zx, tok)
    (xs, ffn_w), zx = both((xs, ffn_w), zx)
    zw1 = go(ffn_w, along(1))
    x_parts = [xs[0]] + zx
    if not fast:
        def regroup(z):
            part = z[..., 192:].reshape(4, 4, shards // 4, 4, out_rows, 192)
            part = jnp.transpose(part, (0, 1, 3, 2, 4, 5)).reshape(4, 4, 192, 192)
            return jnp.concatenate([z[..., :192], part], axis=-1)

        fixed_m, fixed_o = regroup(am), regroup(ao)
        am, ao = jnp.where(c == 1, fixed_m, am), jnp.where(c == 0, fixed_o, ao)

    x, xn, q, kv, a_full, o_full, tok = call(
        qkv_kernel,
        (place, *x_parts, ga, am, ao),
        [row, row, row, sds((2, n, width), BF), sds((4, width, width), BF), sds((width, width), BF)],
        "qkv",
        [SM] + [VM] * 7,
        [VM] * 6,
        deps=[tok, ffn_w],
    )
    kv_other = go(kv, across)
    zw1, tok = tie(zw1, tok)
    p2 = jnp.stack([ffn_half, zw1])
    gs, p2 = both([pick(output_gradient, kk) for kk in range(tps)], p2)
    p2n = send_near(p2)
    zg = [go(gs[kk], along(kk)) for kk in (1, 2)]
    att, full, lse, tok = attend(q, kv, kv_other, bias, 0, 3, (), [tok, p2, *gs])
    (p2n, p1m, zg), tok = tie((p2n, p1m, zg), tok)
    p1m = join_far(p1, p1m)
    p1o = go(p1m, across)
    p2 = join_near(p2, p2n)
    p2m = send_far(p2)
    gs, zg = both(gs, zg)
    zg.append(go(gs[3], along(3)))
    att, full, lse, tok = attend(q, kv, kv_other, bias, 3, 3, (att, full, lse), [tok, p2, p1m, *zg[:2], gs[3]])
    p1o, tok = tie(p1o, tok)
    mid, nf, tok = call(
        project_kernel,
        (x, att, o_full, gf),
        [sds((n, width), F32), row],
        "project",
        [VM] * 4,
        [VM] * 2,
        deps=[tok, p1o],
    )
    (zg[2], p2m), tok = tie((zg[2], p2m), tok)
    g_parts = [gs[0]] + zg
    p2m = join_far(p2, p2m)
    p2o = go(p2m, across)

    out_acc, dnf, keep_a, send_a, tok = ffn_blocks(place, nf, g_parts, p1m, p1o, (), (), 0, 2, [tok, p2m])
    cross_a = go(send_a, across)
    p2o, tok = tie(p2o, tok)
    out_acc, dnf, keep_b, send_b, tok = ffn_blocks(
        place, nf, g_parts, p2m, p2o, (out_acc, dnf), (), 0, 1, [tok, send_a]
    )
    cross_a, tok = tie(cross_a, tok)
    stay_a, leave_a = stage_far(keep_a, cross_a)
    far_a = send_far(leave_a)
    out_acc, dnf, keep_b, send_b, tok = ffn_blocks(
        place, nf, g_parts, p2m, p2o, (out_acc, dnf), (keep_b, send_b), 1, 1, [tok, stay_a, leave_a]
    )
    cross_b = go(send_b, across)
    far_a, tok = tie(far_a, tok)
    stay_a, leave_a = stage_near(stay_a, far_a)
    near_a = send_near(leave_a)

    hid, dmid, dml, da, delta, gf_grad, tok = call(
        turn_kernel,
        (mid, out_acc, dnf, *g_parts, gf, o_full, full),
        [row, sds((n, width), F32), row, row, sds((heads // 2, 2, n), F32), sds((1, width), F32)],
        "turn",
        [VM] * 10,
        [VM] * 6,
        deps=[tok, stay_a, leave_a, send_b],
    )
    (cross_b, near_a), tok = tie((cross_b, near_a), tok)
    blocks_a = stage_last(stay_a, near_a)
    z2 = go(blocks_a[0], along(2))
    stay_b, leave_b = stage_far(keep_b, cross_b)
    far_b = send_far(leave_b)

    def cut_rows(value):
        return [value[128 * k : 128 * k + 128] for k in range(tps)]

    def arrange(pieces):
        stacked = jnp.stack(pieces)
        return jnp.stack([pick(stacked, i) for i in range(tps)])

    hids = cut_rows(hid)
    dq1, dkv1, ds11, tok = attend_back(
        q, da, kv_other, bias[1], 3, 3, lse, delta, (), [tok, stay_b, leave_b, *blocks_a]
    )
    dkv1 = go(dkv1, across)
    (far_b, z2), tok = tie((far_b, z2), tok)
    stay_b, leave_b = stage_near(stay_b, far_b)
    near_b = send_near(leave_b)
    block3, z2 = both(blocks_a[1], z2)
    z3 = go(block3, along(3))
    dq1, own1, ds01, tok = attend_back(
        q, da, kv, bias[0], 3, 3, lse, delta, (dq1,), [tok, stay_b, leave_b, z2, block3]
    )
    (near_b, z3, dkv1), tok = tie((near_b, z3, dkv1), tok)
    blocks_b = stage_last(stay_b, near_b)
    z1 = go(blocks_b[1], along(1))

    keep_v, send_v, up, tok = call(
        partial(weights_kernel, (2, 3), False),
        (place, xn, dq1, own1, dkv1, a_full, att, dml),
        [sds((4, 2, 192, 384), BF), sds((4, 2, 192, 384), BF), sds((n, width), F32)],
        "weights",
        [SM] + [VM] * 7,
        [VM] * 3,
        deps=[tok, *blocks_b, z3],
    )
    if not fast:
        def ungroup(z):
            part = z[..., 192:].reshape(4, 2, 4, shards // 4, out_rows, 192)
            part = jnp.transpose(part, (0, 1, 3, 2, 4, 5)).reshape(4, 2, 192, 192)
            return jnp.concatenate([z[..., :192], part], axis=-1)

        def ungroup_both(keep, send):
            return jnp.where(c == 1, ungroup(keep), keep), jnp.where(c == 0, ungroup(send), send)

        keep_v, send_v = ungroup_both(keep_v, send_v)
    cross_v = go(send_v, across)
    z1, tok = tie(z1, tok)
    hids, z1 = both(hids, z1)
    hid_parts = [go(hids[k], along(k)) for k in (1, 2)]
    dq0, dkv0, ds10, tok = attend_back(
        q, da, kv_other, bias[1], 0, 3, lse, delta, (), [tok, send_v, *hids]
    )
    dkv0 = go(dkv0, across)
    (cross_v, hid_parts), tok = tie((cross_v, hid_parts), tok)
    stay_v, leave_v = stage_far(keep_v, cross_v)
    far_v = send_far(leave_v)
    hids, hid_parts = both(hids, hid_parts)
    hid_parts.append(go(hids[3], along(3)))
    dq0, own0, ds00, tok = attend_back(
        q, da, kv, bias[0], 0, 3, lse, delta, (dq0,), [tok, stay_v, leave_v, *hid_parts[:2], hids[3]]
    )
    (far_v, dkv0, hid_parts[2]), tok = tie((far_v, dkv0, hid_parts[2]), tok)
    stay_v, leave_v = stage_near(stay_v, far_v)
    near_v = send_near(leave_v)
    ffn_mine = ((blocks_b[0].astype(F32) + z1.astype(F32)) + (z2.astype(F32) + z3.astype(F32))).astype(BF)
    keep_w, send_w, back, ga_grad, tok = call(
        partial(weights_kernel, (0, 1), True),
        (place, xn, dq0, own0, dkv0, a_full, att, dml, up, dmid, x, ga),
        [sds((4, 2, 192, 384), BF), sds((4, 2, 192, 384), BF), row, sds((1, width), F32)],
        "weights",
        [SM] + [VM] * 11,
        [VM] * 4,
        deps=[tok, stay_v, leave_v, hid_parts[2], ffn_mine],
    )
    if not fast:
        keep_w, send_w = ungroup_both(keep_w, send_w)
    cross_w = go(send_w, across)
    backs = cut_rows(back)
    back_parts = [go(backs[k], along(k)) for k in (1, 2, 3)]
    near_v, tok = tie(near_v, tok)
    blocks_v = stage_last(stay_v, near_v)
    stay_w, leave_w = stage_far(keep_w, cross_w)
    far_w = send_far(leave_w)
    sums1, tok = bucket_sums(place, 1, buckets_t, (ds10, ds11), [tok, stay_w, leave_w, *blocks_v, *backs])
    (far_w, back_parts), tok = tie((far_w, back_parts), tok)
    stay_w, leave_w = stage_near(stay_w, far_w)
    near_w = send_near(leave_w)
    blocks_v, back_parts = both(blocks_v, back_parts)
    zv = [go(blocks_v[0], along(2)), go(blocks_v[1], along(3))]
    sums0, tok = bucket_sums(place, 0, buckets_t, (ds00, ds01), [tok, stay_w, leave_w, *blocks_v])
    near_w, sums0 = both(near_w, sums0)
    blocks_w = stage_last(stay_w, near_w)
    zw = go(blocks_w[1], along(1))
    sums0, blocks_w = both(sums0, blocks_w)
    hidden_out = arrange([hids[0]] + hid_parts)

    table_sum = jnp.sum((sums0 + sums1).reshape(heads, 16, 16, 32), axis=(1, 2))
    table_abs = jnp.zeros((heads, bias_table.shape[0]), F32).at[head_order].set(table_sum)
    small = jnp.concatenate([ga_grad.reshape(-1), gf_grad.reshape(-1), table_abs.reshape(-1)])
    small = jnp.pad(small, (0, 2048 - small.shape[0])).reshape(16, 128)
    small = small + go(small, across)
    s1, s2, s3 = (go(small, along(k)) for k in (1, 2, 3))
    small = (small + s1) + (s2 + s3)
    if fast:
        s1, s2, s3 = (go(small, lambda a, b, d, k=k: (a ^ k, b, d)) for k in (1, 2, 3))
        small = (small + s1) + (s2 + s3)
    else:
        small = lax.psum(small, "shard")
    small = small.reshape(-1)
    table_grad = small[2 * width : 2 * width + table_abs.size].reshape(table_abs.shape).T

    att_mine = (blocks_w[0].astype(F32) + zw.astype(F32)) + (zv[0].astype(F32) + zv[1].astype(F32))
    mine = jnp.concatenate([ffn_mine, att_mine.astype(BF)[None]])
    lo, hi = both_halves(mine, go(mine, across))
    ffn_lo, ffn_hi, att_lo, att_hi = lo[:2], hi[:2], lo[2], hi[2]
    hidden_grad = arrange([backs[0]] + back_parts).astype(F32)

    out_grad = jnp.concatenate([att_hi[out_rows * i : out_rows * i + out_rows, 192:] for i in range(4)], axis=1)
    return (
        hidden_out,
        hidden_grad,
        small[:width],
        att_lo[:, :192],
        att_lo[:, 192:],
        att_hi[:, :192],
        out_grad,
        table_grad,
        small[width : 2 * width],
        jnp.concatenate([ffn_lo[0], ffn_hi[0]], axis=1),
        jnp.concatenate([ffn_lo[1], ffn_hi[1]], axis=1),
    )


def solution(mesh):
    rows = P("shard", ("ctx", "tp"), None)
    cols = P("shard", "tp")
    both = P(("tp", "shard"), None)
    return jax.shard_map(
        body,
        mesh=mesh,
        in_specs=(rows, P(), cols, cols, cols, both, P(), P(), cols, both, P("ctx", None), rows),
        out_specs=(rows, rows, P(), cols, cols, cols, both, P(), P(), cols, both),
        check_vma=False,
    )
```

```python
from functools import partial

import jax
import jax.numpy as jnp
from jax import lax
from jax.experimental import pallas as pl
from jax.experimental.pallas import tpu as pltpu
from jax.sharding import PartitionSpec as P

EPS = 1e-06
F32 = jnp.float32
BF = jnp.bfloat16
ALL = ("shard", "ctx", "tp")
ORDER = (0, 2, 1, 3)
NN = (((1,), (0,)), ((), ()))
NT = (((1,), (1,)), ((), ()))
TN = (((0,), (0,)), ((), ()))


def dot(a, b, dims=NN):
    return lax.dot_general(a, b, dims, preferred_element_type=F32)


COST = {
    "fence": (60, 1),
    "mark": (0, 1),
    "order": (60, 8),
    "qkv": (60, 16),
    "attend": (60, 18),
    "project": (60, 12),
    "ffn": (60, 20),
    "turn": (60, 16),
    "attend_back": (60, 18),
    "bucket_sums": (60, 16),
    "weights": (60, 16),
}


def call(kernel, args, out_shape, name, in_specs, out_specs, grid=(), scratch=(), deps=(), aliases=None):
    inputs = len(in_specs)
    outputs = inputs + len(deps) + len(out_shape)
    any_space = pl.BlockSpec(memory_space=pl.ANY)

    def wrapped(*refs):
        kernel(*refs[:inputs], *refs[inputs + len(deps) : outputs], *refs[outputs + 1 :])

    cost, room = COST[name]
    return pl.pallas_call(
        wrapped,
        out_shape=[*out_shape, sds((8, 128), F32)],
        grid=grid,
        in_specs=[*in_specs] + [any_space] * len(deps),
        out_specs=[*out_specs, any_space],
        scratch_shapes=scratch,
        compiler_params=pltpu.CompilerParams(vmem_limit_bytes=room * 1024 * 1024),
        input_output_aliases=aliases or {},
        cost_estimate=pl.CostEstimate(
            flops=cost * 1000000000, transcendentals=0, bytes_accessed=cost * 2000000
        ),
        name=name,
    )(*args, *deps)


def fence(*deps):
    return call(lambda: None, (), [], "fence", [], [], deps=jax.tree.leaves(deps))[0]


def mark(*deps):
    return call(lambda: None, (), [], "mark", [], [], deps=jax.tree.leaves(deps))[0]


def in_hbm(value):
    return pltpu.with_memory_space_constraint(value, pltpu.HBM)


VM = pl.BlockSpec(memory_space=pltpu.VMEM)
SM = pl.BlockSpec(memory_space=pltpu.SMEM)


def whole(*shape):
    return pl.BlockSpec(shape, lambda *_: (0,) * len(shape))


def sds(shape, dtype):
    return jax.ShapeDtypeStruct(shape, dtype)


def order_kernel(place, buckets_ref, out_ref):
    tp = place[0]
    queries, keys = buckets_ref.shape
    per = keys // 256
    for j in range(keys // 128):
        block = (place[1] ^ (j // per)) * per + (tp ^ (j % per))
        cols = pl.ds(pl.multiple_of(block * 128, 128), 128)
        for k in range(queries // 128):
            rows = pl.ds(pl.multiple_of((tp ^ k) * 128, 128), 128)
            out_ref[128 * j : 128 * j + 128, 128 * k : 128 * k + 128] = buckets_ref[rows, cols].T


def order_buckets(place, buckets, deps):
    shape = (buckets.shape[1], buckets.shape[0])
    return call(order_kernel, (place, buckets), [sds(shape, jnp.int32)], "order", [SM, VM], [VM], deps=deps)


def look_up(table_ref, head, index):
    row = jnp.broadcast_to(table_ref[pl.ds(head, 1), :], (index.shape[0], 128))
    parts = [
        jnp.take_along_axis(row, index[:, 128 * k : 128 * k + 128], axis=1, mode="promise_in_bounds")
        for k in range(index.shape[1] // 128)
    ]
    return jnp.concatenate(parts, axis=1)


def qkv_kernel(place, x0, x1, x2, x3, gain, mine, other, x_out, xn_out, q_out, kv_out, a_out, o_out):
    first = place[1] == 0
    for r, ref in enumerate((x0, x1, x2, x3)):
        x = ref[...]
        x_out[128 * r : 128 * r + 128, :] = x
        xf = x.astype(F32)
        scale = lax.rsqrt(jnp.mean(xf * xf, axis=-1, keepdims=True) + EPS)
        xn_out[128 * r : 128 * r + 128, :] = (xf * scale * gain[...]).astype(BF)
    for k in range(4):
        for s in range(4):
            m = mine[place[2 + s], k]
            o = other[place[6 + s], k]
            a_out[k, 192 * s : 192 * s + 192, 0:384] = jnp.where(first, m, o)
            a_out[k, 192 * s : 192 * s + 192, 384:768] = jnp.where(first, o, m)
        for s in range(4):
            for c in range(4):
                o_out[192 * k + 48 * s : 192 * k + 48 * s + 48, 192 * c : 192 * c + 192] = a_out[
                    k, 192 * s + 48 * c : 192 * s + 48 * c + 48, 576:768
                ]
        y = dot(xn_out[...], a_out[k, :, 0:576]).astype(BF)
        q_out[:, 192 * k : 192 * k + 192] = y[:, 0:192]
        kv_out[0, :, 192 * k : 192 * k + 192] = y[:, 192:384]
        kv_out[1, :, 192 * k : 192 * k + 192] = y[:, 384:576]


def lanes_of(pair):
    return pl.ds(pl.multiple_of(128 * pair, 128), 128)


def attend_kernel(begin, q_ref, own, other, labels, table, *refs):
    att_ref, full_ref, lse_ref = refs[-3:]
    pair = pl.program_id(0) + begin
    cols = lanes_of(pair)
    part_keys = own.shape[1] // 2
    qt = q_ref[:, cols].T
    vts = [own[1, :, cols].T, other[1, :, cols].T]
    side = lax.broadcasted_iota(jnp.int32, qt.shape, 0) // 64
    ones = jnp.ones((16, part_keys), BF)
    results = []
    for h in range(2):
        q = jnp.where(side == h, qt, jnp.zeros((), BF))
        scores = []
        top = None
        for i in range(4):
            rows = slice(part_keys * (i % 2), part_keys * (i % 2 + 1))
            bias = look_up(table, 2 * pair + h, labels[part_keys * i : part_keys * (i + 1), :])
            score = dot((own, other)[i // 2][0, rows, cols], q) + bias
            high = jnp.max(score, axis=0, keepdims=True)
            top = high if i == 0 else jnp.maximum(top, high)
            scores.append(score)
        part = None
        for i, score in enumerate(scores):
            values = vts[i // 2][64 * h : 64 * h + 64, part_keys * (i % 2) : part_keys * (i % 2 + 1)]
            e = jnp.exp(score - top).astype(BF)
            piece = dot(jnp.concatenate([values, ones], axis=0), e)
            part = piece if i == 0 else part + piece
        total = part[64:65, :]
        lse_ref[pair, h : h + 1, :] = top + jnp.log(total)
        results.append(part[0:64, :] / total)
    full = jnp.concatenate(results, axis=0).T
    full_ref[:, cols] = full
    att_ref[:, cols] = full.astype(BF)


def attend(q, own, other, labels, table, begin, pairs, before, deps):
    rows, width = q.shape
    return call(
        partial(attend_kernel, begin),
        (q, own, other, labels, table, *before),
        [sds((rows, width), BF), sds((rows, width), F32), sds((width // 128, 2, rows), F32)],
        "attend",
        [VM] * (5 + len(before)),
        [VM] * 3,
        grid=(pairs,),
        deps=deps,
        aliases={5: 0, 6: 1, 7: 2} if before else None,
    )


def project_kernel(x_ref, att_ref, o_ref, gain, mid_ref, nf_ref):
    mid = x_ref[...].astype(F32) + dot(att_ref[...], o_ref[...])
    mid_ref[...] = mid
    scale = lax.rsqrt(jnp.mean(mid * mid, axis=-1, keepdims=True) + EPS)
    nf_ref[...] = (mid * scale * gain[...]).astype(BF)


def ffn_kernel(first_call, begin, place, nf_ref, g0, g1, g2, g3, mine, other, *refs):
    if first_call:
        out_ref, dnf_ref, keep, send, w1s, w2s, gs, us, ds = refs
    else:
        out_in, dnf_in = refs[:2]
        out_ref, dnf_ref, keep, send, w1s, w2s, gs, us, ds = refs[-9:]
    first = place[1] == 0
    step = pl.program_id(0)
    block = step + begin

    @pl.when(step == 0)
    def _():
        for r, ref in enumerate((g0, g1, g2, g3)):
            gs[128 * r : 128 * r + 128, :] = ref[...]
        if first_call:
            out_ref[...] = jnp.zeros_like(out_ref)
            dnf_ref[...] = jnp.zeros_like(dnf_ref)
        else:
            out_ref[...] = out_in[...]
            dnf_ref[...] = dnf_in[...]

    for s in range(4):
        rows = slice(192 * s, 192 * s + 192)
        for i, w in enumerate((w1s, w2s)):
            m = mine[place[2 + s], block, i]
            o = other[place[6 + s], block, i]
            w[rows, 0:384] = jnp.where(first, m, o)
            w[rows, 384:768] = jnp.where(first, o, m)
    for j in range(3):
        cols = slice(256 * j, 256 * j + 256)
        v = dot(nf_ref[...], w1s[:, cols])
        square = v * v
        th = jnp.tanh(v * (0.7978845608 + (0.7978845608 * 0.044715) * square))
        half = 0.5 + 0.5 * th
        us[:, cols] = (v * half).astype(BF)
        slope = half + v * (0.5 - 0.5 * th * th) * (0.7978845608 + (0.7978845608 * 3 * 0.044715) * square)
        ds[:, cols] = (dot(gs[...], w2s[cols, :], NT) * slope).astype(BF)
    out_ref[...] += dot(us[...], w2s[...])
    dnf_ref[...] += dot(ds[...], w1s[...], NT)
    d1 = dot(nf_ref[...], ds[...], TN).astype(BF)
    d2 = dot(us[...], gs[...], TN).astype(BF)
    for s in range(4):
        rows = slice(192 * s, 192 * s + 192)
        for i, d in enumerate((d1, d2)):
            lo = d[rows, 0:384]
            hi = d[rows, 384:768]
            keep[place[2 + s], block, i] = jnp.where(first, lo, hi)
            send[place[6 + s], block, i] = jnp.where(first, hi, lo)


def ffn_blocks(place, nf, g, mine, other, carry, grads, begin, count, deps):
    rows, width = nf.shape
    aliases = {}
    if carry:
        aliases = {8: 0, 9: 1}
    if grads:
        aliases.update({10: 2, 11: 3})
    return call(
        partial(ffn_kernel, not carry, begin),
        (place, nf, *g, mine, other, *carry, *grads),
        [sds((rows, width), F32), sds((rows, width), F32)] + [sds(mine.shape, BF)] * 2,
        "ffn",
        [SM] + [VM] * (7 + len(carry) + len(grads)),
        [VM] * 4,
        grid=(count,),
        scratch=[pltpu.VMEM((width, width), BF)] * 2 + [pltpu.VMEM((rows, width), BF)] * 3,
        deps=deps,
        aliases=aliases,
    )


def store_gain(ref, value):
    for i in range(ref.shape[0]):
        ref[i : i + 1, :] = value[:, 128 * i : 128 * i + 128]


def turn_kernel(mid_ref, out_in, dnf_in, g0, g1, g2, g3, gain, o_ref, full_ref, h0, h1, h2, h3, dmid_ref, dml_ref, da_ref, delta_ref, gg_ref):
    mid = mid_ref[...]
    hid = (mid + out_in[...]).astype(BF)
    for r, ref in enumerate((h0, h1, h2, h3)):
        ref[...] = hid[128 * r : 128 * r + 128, :]
    scale = lax.rsqrt(jnp.mean(mid * mid, axis=-1, keepdims=True) + EPS)
    up = dnf_in[...]
    weighted = up * gain[...]
    mean_term = jnp.mean(weighted * mid, axis=-1, keepdims=True)
    res = scale * weighted - mid * (scale * scale * scale) * mean_term
    store_gain(gg_ref, jnp.sum(up * mid * scale, axis=0, keepdims=True))
    for r, ref in enumerate((g0, g1, g2, g3)):
        rows = slice(128 * r, 128 * r + 128)
        dmid_ref[rows, :] = res[rows, :] + ref[...].astype(F32)
    low = dmid_ref[...].astype(BF)
    dml_ref[...] = low
    da = dot(low, o_ref[...], NT).astype(BF)
    da_ref[...] = da
    pairs = delta_ref.shape[0]
    width = da.shape[1]
    head = lax.broadcasted_iota(jnp.int32, (2 * pairs, width), 0)
    lane = lax.broadcasted_iota(jnp.int32, (2 * pairs, width), 1)
    pick = jnp.where(lane // 64 == head, 1.0, 0.0)
    delta = lax.dot_general(
        pick, da.astype(F32) * full_ref[...], NT, precision=lax.Precision.HIGHEST, preferred_element_type=F32
    )
    for p in range(pairs):
        delta_ref[p] = delta[2 * p : 2 * p + 2, :]


def split_rows(value):
    row = lax.broadcasted_iota(jnp.int32, (64, value.shape[1]), 0)
    out = jnp.zeros((64, value.shape[1]), BF)
    for i in range(3):
        piece = value.astype(BF)
        out = jnp.where(row == i, piece, out)
        value = value - piece.astype(F32)
    return out


def attend_back_kernel(begin, half, last, q_ref, da_ref, kv_ref, labels, table, lse_ref, delta_ref, *refs):
    if last:
        dq_in, dq_ref, dkv_ref, ds_ref = refs
    else:
        dq_ref, dkv_ref, ds_ref = refs
    pair = pl.program_id(0) + begin
    cols = lanes_of(pair)
    outs = lanes_of(pl.program_id(0))
    part_keys = kv_ref.shape[1] // 2
    zero = jnp.zeros((), BF)
    q_all, da_all = q_ref[:, cols], da_ref[:, cols]
    qt = q_all.T
    dat = da_all.T
    kt = kv_ref[0, :, cols].T
    lane = lax.broadcasted_iota(jnp.int32, (1, 128), 1)
    dqs = [None, None]
    qs, das, qas, daas = [], [], [], []
    for h in range(2):
        own = lane // 64 == h
        qs.append(jnp.where(own, q_all, zero))
        das.append(jnp.where(own, da_all, zero))
        for t, stat, out in ((qt, lse_ref, qas), (dat, delta_ref, daas)):
            extra = split_rows(stat[pair, h : h + 1, :])
            mine = t[64 * h : 64 * h + 64, :]
            out.append(jnp.concatenate([mine, extra] if h == 0 else [extra, mine], axis=0))
    for i in range(2):
        rows = slice(part_keys * i, part_keys * (i + 1))
        k = kv_ref[0, rows, cols]
        v = kv_ref[1, rows, cols]
        dk = dv = None
        for h in range(2):
            own = lane // 64 == h
            minus = jnp.where(lane % 64 < 3, -1.0, 0.0).astype(BF)
            first = half * kv_ref.shape[1] + part_keys * i
            bias = look_up(table, 2 * pair + h, labels[first : first + part_keys, :])
            p = jnp.exp(dot(jnp.where(own, k, minus), qas[h]) + bias)
            ds = (p * dot(jnp.where(own, v, minus), daas[h])).astype(BF)
            ds_ref[h, rows, :] = ds
            a = dot(kt[64 * h : 64 * h + 64, rows], ds)
            b = dot(ds, qs[h])
            c = dot(p.astype(BF), das[h])
            dqs[h] = a if i == 0 else dqs[h] + a
            dk, dv = (b, c) if h == 0 else (dk + b, dv + c)
        dkv_ref[0, rows, outs] = dk.astype(dkv_ref.dtype)
        dkv_ref[1, rows, outs] = dv.astype(dkv_ref.dtype)
    dq = jnp.concatenate(dqs, axis=0).T
    if last:
        dq_ref[:, outs] = (dq_in[:, outs] + dq).astype(dq_ref.dtype)
    else:
        dq_ref[:, outs] = dq


def attend_back(q, da, kv, labels, table, half, begin, pairs, lse, delta, dq, deps):
    rows = q.shape[0]
    width = 128 * pairs
    keys = kv.shape[1]
    last = len(dq) > 0
    return call(
        partial(attend_back_kernel, begin, half, last),
        (q, da, kv, labels, table, lse, delta, *dq),
        [
            sds((rows, width), BF if last else F32),
            sds((2, keys, width), F32 if last else BF),
            pltpu.HBM((2 * pairs, keys, rows), BF),
        ],
        "attend_back",
        [VM] * (7 + len(dq)),
        [VM, VM, pl.BlockSpec((2, keys, rows), lambda p: (p, 0, 0))],
        grid=(pairs,),
        deps=deps,
    )


def weights_kernel(blocks, last, place, xn_ref, dq_ref, dkv_in, dkv_add, a_ref, att_ref, dml_ref, *refs):
    if last:
        up_in, dmid_ref, x_ref, gain, keep, send, h0, h1, h2, h3, gg_ref = refs
        up = up_in[...]
    else:
        keep, send, up_ref = refs
        up = None
    first = place[1] == 0
    dq = dq_ref[...]
    dk, dv = ((dkv_in[i] + dkv_add[i].astype(F32)).astype(BF) for i in range(2))
    xn = xn_ref[...]
    for i, k in enumerate(blocks):
        cols = slice(192 * i, 192 * i + 192)
        cat = jnp.concatenate([dq[:, cols], dk[:, cols], dv[:, cols]], axis=1)
        part = dot(cat, a_ref[k, :, 0:576], NT)
        up = part if up is None else up + part
        grad = dot(xn, cat, TN).astype(BF)
        out = dot(att_ref[:, 192 * k : 192 * k + 192], dml_ref[...], TN).astype(BF)
        for s in range(4):
            rows = slice(192 * s, 192 * s + 192)
            lo = grad[rows, 0:384]
            piece = jnp.concatenate(
                [out[48 * s : 48 * s + 48, 192 * c : 192 * c + 192] for c in range(4)], axis=0
            )
            hi = jnp.concatenate([grad[rows, 384:576], piece], axis=1)
            keep[place[2 + s], i] = jnp.where(first, lo, hi)
            send[place[6 + s], i] = jnp.where(first, hi, lo)
    if not last:
        up_ref[...] = up
        return
    x = x_ref[...].astype(F32)
    scale = lax.rsqrt(jnp.mean(x * x, axis=-1, keepdims=True) + EPS)
    weighted = up * gain[...]
    mean_term = jnp.mean(weighted * x, axis=-1, keepdims=True)
    res = scale * weighted - x * (scale * scale * scale) * mean_term
    store_gain(gg_ref, jnp.sum(up * x * scale, axis=0, keepdims=True))
    back = (dmid_ref[...] + res).astype(BF)
    for r, ref in enumerate((h0, h1, h2, h3)):
        ref[...] = back[128 * r : 128 * r + 128, :]


def bucket_kernel(source, adds, place, labels, ds0_ref, ds1_ref, *refs):
    before = refs[0] if adds else None
    out_ref, acc, table = refs[-3:]
    tp = place[0]
    step = pl.program_id(0)
    heads, group, queries = ds0_ref.shape
    first = source * (labels.shape[0] // 2) + step * group

    @pl.when(step == 0)
    def _():
        acc[...] = jnp.zeros_like(acc)

    label = [(lax.broadcasted_iota(jnp.int32, (16, 128), 0) + 16 * i).astype(F32).astype(BF) for i in range(2)]
    one, zero = jnp.ones((), BF), jnp.zeros((), BF)
    for g in range(group // 16):
        for k in range(queries // 128):
            index = labels[pl.ds(pl.multiple_of(first + 16 * g, 16), 16), 128 * k : 128 * k + 128].astype(F32)
            for j in range(16):
                spread = jnp.broadcast_to(index[j : j + 1, :], (16, 128)).astype(BF)
                for i in range(2):
                    at = 32 * j + 16 * i
                    table[at : at + 16, 128 * k : 128 * k + 128] = jnp.where(spread == label[i], one, zero)
        left = [d[:, 16 * g : 16 * g + 16, :].reshape(heads * 16, queries) for d in (ds0_ref, ds1_ref)]
        acc[...] += dot(jnp.concatenate(left, axis=0), table[...], NT)

    @pl.when(step == pl.num_programs(0) - 1)
    def _():
        row = lax.broadcasted_iota(jnp.int32, acc.shape, 0) % 16
        col = lax.broadcasted_iota(jnp.int32, acc.shape, 1) // 32
        hit = jnp.where(row == col, acc[...], 0.0)
        fold = (hit[:, 0:128] + hit[:, 128:256]) + (hit[:, 256:384] + hit[:, 384:512])
        sums = jnp.sum(fold.reshape(2 * heads, 16, 128), axis=1)
        sums = sums + pltpu.roll(sums, 64, 1)
        sums = sums + pltpu.roll(sums, 32, 1)
        lane = lax.broadcasted_iota(jnp.int32, sums.shape, 1)
        sums = jnp.where(lane < 32, sums, 0.0)
        out_ref[...] = jnp.zeros_like(out_ref) if before is None else before[...]
        each = heads // 2
        for k in range(4):
            for h in range(each):
                at = (tp ^ ORDER[k]) * each + h
                out_ref[pl.ds(at, 1), :] = out_ref[pl.ds(at, 1), :] + sums[each * k + h : each * k + h + 1, :]


def bucket_sums(place, half, labels, ds, before, deps):
    heads, keys, queries = ds[0].shape
    spec = pl.BlockSpec((heads, 128, queries), lambda j: (0, j, 0))
    return call(
        partial(bucket_kernel, half, len(before)),
        (place, labels, in_hbm(ds[0]), in_hbm(ds[1]), *before),
        [sds((16, 128), F32)],
        "bucket_sums",
        [SM, VM, spec, spec] + [VM] * len(before),
        [VM],
        grid=(keys // 128,),
        scratch=[pltpu.VMEM((heads * 32, 512), F32), pltpu.VMEM((512, queries), BF)],
        deps=deps,
    )


def move(value, move_to, sizes):
    shards, ctx, tps = sizes
    pairs = []
    for s in range(shards):
        for c in range(ctx):
            for t in range(tps):
                a, b, d = move_to(s, c, t)
                pairs.append(((s * ctx + c) * tps + t, (a * ctx + b) * tps + d))
    return lax.ppermute(value, ALL, pairs)


def body(
    hidden_in,
    norm_attn_gain,
    query_weight,
    key_weight,
    value_weight,
    out_weight,
    bias_table,
    norm_ffn_gain,
    ffn_in_weight,
    ffn_out_weight,
    buckets,
    output_gradient,
):
    sizes = tuple(lax.axis_size(a) for a in ALL)
    shards, ctxs, tps = sizes
    s, c, t = (lax.axis_index(a) for a in ALL)
    fast = shards == 4
    assert ctxs == 2 and tps == 4 and hidden_in.shape[0] == tps
    heads = bias_table.shape[1]

    def along(k):
        return lambda a, b, d: (a, b, d ^ k)

    def across(a, b, d):
        return (a, 1 - b, d)

    def near(a, b, d):
        return (a ^ (1 if b == 0 else 2), b, d)

    def far(a, b, d):
        return (a ^ (2 if b == 0 else 1), b, d)

    go = partial(move, sizes=sizes)

    def spot(shard, core):
        d = shard ^ s
        return jnp.where(core == 0, d, (d >> 1) | ((d & 1) << 1)) if fast else jnp.int32(shard)

    place = jnp.stack(
        [t, c] + [spot(i, c) for i in range(4)] + [spot(i, 1 - c) for i in range(4)]
    ).astype(jnp.int32)

    def pick(value, k):
        return lax.dynamic_index_in_dim(value, t ^ k, 0, keepdims=False)

    def tie(value, token):
        return lax.optimization_barrier((value, token))

    def add(a, b):
        return (a.astype(F32) + b.astype(F32)).astype(BF)

    def send_near(value):
        return go(value, near) if fast else value

    def send_far(value):
        return go(value, far) if fast else value

    def join_near(value, got):
        return jnp.stack([value, got]) if fast else value

    def join_far(value, got):
        if fast:
            return jnp.concatenate([value, got])
        full = lax.all_gather(value, "shard", axis=0, tiled=False)
        full = jnp.moveaxis(full, 0, -3)
        lead = full.shape[:-3]
        return jnp.moveaxis(full.reshape(lead + (4, 192, 384)), -3, 0)

    def stage_far(keep, got):
        if fast:
            return add(keep[:2], got[:2]), add(keep[2:], got[2:])
        return add(keep, got), jnp.zeros((8, 128), BF)

    def stage_near(stay, got):
        return (add(stay[0], got[0]), add(stay[1], got[1])) if fast else (stay, got)

    def stage_last(stay, got):
        if fast:
            return [add(stay[i], got[i]) for i in range(stay.shape[0])]
        total = jnp.moveaxis(stay, 0, -3)
        lead = total.shape[:-3]
        total = jnp.moveaxis(total.reshape(lead + (shards, 768 // shards, 384)), -3, 0)
        total = lax.psum_scatter(total, "shard", scatter_dimension=0, tiled=False)
        return [total[i] for i in range(total.shape[0])]

    def my_half(lo, hi):
        return jnp.where(c == 0, lo, hi)

    def both_halves(mine, other):
        return jnp.where(c == 0, mine, other).astype(F32), jnp.where(c == 0, other, mine).astype(F32)

    width = hidden_in.shape[2]
    n = 512
    ga = norm_attn_gain.reshape(1, width)
    gf = norm_ffn_gain.reshape(1, width)
    row = sds((n, width), BF)
    out_rows = out_weight.shape[0]

    out_pack = jnp.concatenate([out_weight[:, 192 * i : 192 * i + 192] for i in range(4)], axis=0)
    att_half = my_half(
        jnp.concatenate([query_weight, key_weight], axis=1), jnp.concatenate([value_weight, out_pack], axis=1)
    )
    ffn_half = my_half(
        jnp.stack([ffn_in_weight[:, :384], ffn_out_weight[:, :384]]),
        jnp.stack([ffn_in_weight[:, 384:], ffn_out_weight[:, 384:]]),
    )
    head_order = jnp.concatenate([(t ^ k) * (heads // tps) + jnp.arange(heads // tps) for k in ORDER])
    table_rel = jnp.pad(jnp.take(bias_table.T, head_order, axis=0), ((0, 0), (0, 128 - bias_table.shape[0])))

    def both(value, token):
        return lax.optimization_barrier((value, token))

    pair = jnp.stack([att_half, go(att_half, along(2))])
    a0 = go(pair, along(1))
    xs = [pick(hidden_in, k) for k in range(tps)]
    labels, tok = order_buckets(place, buckets, [pair, *xs])
    a0, tok = tie(a0, tok)
    a0 = jnp.concatenate([pair, a0])
    a1 = send_near(a0)
    xs, a0 = both(xs, a0)
    zx = [go(xs[k], along(k)) for k in (1, 2, 3)]
    tok = fence(tok, a0, *xs)
    a1, tok = tie(a1, tok)
    a1 = join_near(a0, a1)
    am = send_far(a1)
    tok = fence(tok, a1)
    zx, tok = tie(zx, tok)
    ffn_w, zx = both(ffn_half, zx)
    w2 = go(ffn_w, along(2))
    tok = mark(tok, ffn_w)
    am, tok = tie(am, tok)
    am = join_far(a1, am)
    ao = go(am, across)
    w2, am = both(w2, am)
    pa = jnp.stack([ffn_half, w2])
    pb = go(pa, along(1))
    pan = send_near(pa)
    tok = fence(tok, am, pa)
    x_parts = [xs[0]] + zx
    if not fast:
        def regroup(z):
            part = z[..., 192:].reshape(4, 4, shards // 4, 4, out_rows, 192)
            part = jnp.transpose(part, (0, 1, 3, 2, 4, 5)).reshape(4, 4, 192, 192)
            return jnp.concatenate([z[..., :192], part], axis=-1)

        fixed_m, fixed_o = regroup(am), regroup(ao)
        am, ao = jnp.where(c == 1, fixed_m, am), jnp.where(c == 0, fixed_o, ao)

    x, xn, q, kv, a_full, o_full, tok = call(
        qkv_kernel,
        (place, *x_parts, ga, am, ao),
        [row, row, row, sds((2, n, width), BF), sds((4, width, width), BF), sds((width, width), BF)],
        "qkv",
        [SM] + [VM] * 7,
        [VM] * 6,
        deps=[tok],
    )
    kv_other = go(kv, across)
    tok = mark(tok, kv)
    (pan, pb), tok = tie((pan, pb), tok)
    pa = join_near(pa, pan)
    pam = send_far(pa)
    pbn = send_near(pb)
    gs, pa = both([pick(output_gradient, kk) for kk in range(tps)], pa)
    zg = [go(gs[kk], along(kk)) for kk in (1, 2)]
    tok = fence(tok, pa, pb, gs)
    kv_other, tok = tie(kv_other, tok)
    att, full, lse, tok = attend(q, kv, kv_other, labels, table_rel, 0, 3, (), [tok])
    (pam, pbn, zg), tok = tie((pam, pbn, zg), tok)
    pam = join_far(pa, pam)
    pao = go(pam, across)
    pb = join_near(pb, pbn)
    pbm = send_far(pb)
    g3, pb = both(gs[3], pb)
    zg.append(go(g3, along(3)))
    att, full, lse, tok = attend(q, kv, kv_other, labels, table_rel, 3, 3, (att, full, lse), [tok, pam, pb, g3])
    (pao, pbm), tok = tie((pao, pbm), tok)
    pbm = join_far(pb, pbm)
    pbo = go(pbm, across)
    mid, nf, tok = call(
        project_kernel,
        (x, att, o_full, gf),
        [sds((n, width), F32), row],
        "project",
        [VM] * 4,
        [VM] * 2,
        deps=[tok, pao, pbm],
    )
    zg[2], tok = tie(zg[2], tok)
    g_parts = [gs[0]] + zg

    out_acc, dnf, keep_a, send_a, tok = ffn_blocks(place, nf, g_parts, pam, pao, (), (), 0, 2, [tok])
    cross_a = go(send_a, across)
    pbo, tok = tie(pbo, tok)
    out_acc, dnf, keep_b, send_b, tok = ffn_blocks(
        place, nf, g_parts, pbm, pbo, (out_acc, dnf), (), 0, 1, [tok, send_a]
    )
    cross_a, tok = tie(cross_a, tok)
    stay_a, leave_a = stage_far(keep_a, cross_a)
    far_a = send_far(leave_a)
    out_acc, dnf, keep_b, send_b, tok = ffn_blocks(
        place, nf, g_parts, pbm, pbo, (out_acc, dnf), (keep_b, send_b), 1, 1, [tok, stay_a, leave_a]
    )
    cross_b = go(send_b, across)

    piece = sds((n // tps, width), BF)
    gain_rows = sds((width // 128, 128), F32)
    *hids, dmid, dml, da, delta, gf_grad, tok = call(
        turn_kernel,
        (mid, out_acc, dnf, *g_parts, gf, o_full, full),
        [piece] * 4 + [sds((n, width), F32), row, row, sds((heads // 2, 2, n), F32), gain_rows],
        "turn",
        [VM] * 10,
        [VM] * 9,
        deps=[tok, send_b],
    )

    def arrange(pieces):
        stacked = jnp.stack(pieces)
        return jnp.stack([pick(stacked, i) for i in range(tps)])

    hid_parts = [go(hids[k], along(k)) for k in (1, 2, 3)]
    (cross_b, far_a), tok = tie((cross_b, far_a), tok)
    stay_a, leave_a = stage_near(stay_a, far_a)
    near_a = send_near(leave_a)
    stay_b, leave_b = stage_far(keep_b, cross_b)
    far_b = send_far(leave_b)
    dq1, dkv1, ds11, tok = attend_back(
        q, da, kv_other, labels, table_rel, 1, 3, 3, lse, delta, (), [tok, stay_b, leave_b, stay_a, leave_a, *hids]
    )
    dkv1 = go(dkv1, across)
    first_hids, tok = tie(hid_parts[:2], tok)
    hid_parts = [*first_hids, hid_parts[2]]
    dq1, own1, ds01, tok = attend_back(
        q, da, kv, labels, table_rel, 0, 3, 3, lse, delta, (dq1,), [tok]
    )
    (near_a, far_b, dkv1, hid_parts[2]), tok = tie((near_a, far_b, dkv1, hid_parts[2]), tok)
    blocks_a = stage_last(stay_a, near_a)
    stay_b, leave_b = stage_near(stay_b, far_b)
    near_b = send_near(leave_b)

    keep_v, send_v, up, tok = call(
        partial(weights_kernel, (2, 3), False),
        (place, xn, dq1, own1, dkv1, a_full, att, dml),
        [sds((4, 2, 192, 384), BF), sds((4, 2, 192, 384), BF), sds((n, width), F32)],
        "weights",
        [SM] + [VM] * 7,
        [VM] * 3,
        deps=[tok, stay_b, leave_b, *blocks_a, *hid_parts],
    )
    if not fast:
        def ungroup(z):
            part = z[..., 192:].reshape(4, 2, 4, shards // 4, out_rows, 192)
            part = jnp.transpose(part, (0, 1, 3, 2, 4, 5)).reshape(4, 2, 192, 192)
            return jnp.concatenate([z[..., :192], part], axis=-1)

        def ungroup_both(keep, send):
            return jnp.where(c == 1, ungroup(keep), keep), jnp.where(c == 0, ungroup(send), send)

        keep_v, send_v = ungroup_both(keep_v, send_v)
    cross_v = go(send_v, across)
    near_b, tok = tie(near_b, tok)
    blocks_b = jnp.stack(stage_last(stay_b, near_b))
    zb = go(blocks_b, along(1))
    dq0, dkv0, ds10, tok = attend_back(
        q, da, kv_other, labels, table_rel, 1, 0, 3, lse, delta, (), [tok, send_v, blocks_b]
    )
    dkv0 = go(dkv0, across)
    cross_v, tok = tie(cross_v, tok)
    stay_v, leave_v = stage_far(keep_v, cross_v)
    far_v = send_far(leave_v)
    dq0, own0, ds00, tok = attend_back(
        q, da, kv, labels, table_rel, 0, 0, 3, lse, delta, (dq0,), [tok, stay_v, leave_v]
    )
    (far_v, dkv0, zb), tok = tie((far_v, dkv0, zb), tok)
    c0, c2 = add(blocks_a[0], zb[0]), add(blocks_a[1], zb[1])
    zc = go(c2, along(2))
    stay_v, leave_v = stage_near(stay_v, far_v)
    near_v = send_near(leave_v)
    sums, tok = bucket_sums(place, 1, labels, (ds10, ds11), (), [tok, stay_v, leave_v, dkv0, c0, c2])
    near_v, tok = tie(near_v, tok)
    blocks_v = jnp.stack(stage_last(stay_v, near_v))
    zv = go(blocks_v, along(1))
    keep_w, send_w, *backs, ga_grad, tok = call(
        partial(weights_kernel, (0, 1), True),
        (place, xn, dq0, own0, dkv0, a_full, att, dml, up, dmid, x, ga),
        [sds((4, 2, 192, 384), BF)] * 2 + [piece] * 4 + [gain_rows],
        "weights",
        [SM] + [VM] * 11,
        [VM] * 7,
        deps=[tok, blocks_v],
    )
    if not fast:
        keep_w, send_w = ungroup_both(keep_w, send_w)
    cross_w = go(send_w, across)
    zc, tok = tie(zc, tok)
    ffn_mine = add(c0, zc)
    back_parts = [backs[0]] + [go(backs[k], along(k)) for k in (1, 2)]
    tok = fence(tok, backs, send_w, ffn_mine)
    cross_w, tok = tie(cross_w, tok)
    stay_w, leave_w = stage_far(keep_w, cross_w)
    far_w = send_far(leave_w)
    sums, tok = bucket_sums(place, 0, labels, (ds00, ds01), (sums,), [tok, stay_w, leave_w])
    (far_w, zv, got_backs), tok = tie((far_w, zv, back_parts), tok)
    ffn_mine, zv = both(ffn_mine, zv)
    ffn_other = go(ffn_mine, across)
    stay_w, leave_w = stage_near(stay_w, far_w)
    near_w = send_near(leave_w)
    back3 = go(backs[3], along(3))
    small = jnp.concatenate([sums, jnp.pad(ga_grad, ((0, 2), (0, 0))), jnp.pad(gf_grad, ((0, 2), (0, 0)))])
    got = go(small, across)
    tok = fence(tok, stay_w, leave_w, small, ffn_mine)
    (got, ffn_other), tok = tie((got, ffn_other), tok)
    small = small + got
    ffn_lo, ffn_hi = both_halves(ffn_mine, ffn_other)
    if fast:
        got = go(small, lambda a, b, d: (a ^ 1, b, d))
        tok = fence(tok, small)
        (got, near_w), tok = tie((got, near_w), tok)
        small = small + got
        got = go(small, lambda a, b, d: (a ^ 2, b, d))
    else:
        small = lax.psum(small, "shard")
    blocks_w = stage_last(stay_w, near_w)
    d0, d2 = add(blocks_w[0], zv[0]), add(blocks_w[1], zv[1])
    zw = go(d2, along(2))
    w1_grad = jnp.concatenate([ffn_lo[0], ffn_hi[0]], axis=1)
    w2_grad = jnp.concatenate([ffn_lo[1], ffn_hi[1]], axis=1)
    tok = fence(tok, small, d0, d2, w1_grad, w2_grad)
    if fast:
        got, tok = tie(got, tok)
        small = small + got
    got = go(small, along(1))
    tok = fence(tok, small)
    (got, zw, back3), tok = tie((got, zw, back3), tok)
    small = small + got
    got = go(small, along(2))
    att_mine = add(d0, zw)
    att_other = go(att_mine, across)
    hidden_grad = arrange([*got_backs, back3]).astype(F32)
    tok = fence(tok, small, att_mine, hidden_grad)
    (got, att_other), tok = tie((got, att_other), tok)
    small = small + got
    hidden_out = arrange([hids[0]] + hid_parts)
    table_grad = small[:heads, : bias_table.shape[0]].T
    gains = width // 128

    att_lo, att_hi = both_halves(att_mine, att_other)
    out_grad = jnp.concatenate([att_hi[out_rows * i : out_rows * i + out_rows, 192:] for i in range(4)], axis=1)
    return (
        hidden_out,
        hidden_grad,
        small[16 : 16 + gains].reshape(width),
        att_lo[:, :192],
        att_lo[:, 192:],
        att_hi[:, :192],
        out_grad,
        table_grad,
        small[24 : 24 + gains].reshape(width),
        w1_grad,
        w2_grad,
    )


def solution(mesh):
    rows = P("shard", ("ctx", "tp"), None)
    cols = P("shard", "tp")
    both = P(("tp", "shard"), None)
    return jax.shard_map(
        body,
        mesh=mesh,
        in_specs=(rows, P(), cols, cols, cols, both, P(), P(), cols, both, P("ctx", None), rows),
        out_specs=(rows, rows, P(), cols, cols, cols, both, P(), P(), cols, both),
        check_vma=False,
    )
```

```python
from functools import partial

import jax
import jax.numpy as jnp
from jax import lax
from jax.experimental import pallas as pl
from jax.experimental.pallas import tpu as pltpu
from jax.sharding import PartitionSpec as P

EPS = 1e-06
F32 = jnp.float32
BF = jnp.bfloat16
ALL = ("shard", "ctx", "tp")
ORDER = (0, 2, 1, 3)
NN = (((1,), (0,)), ((), ()))
NT = (((1,), (1,)), ((), ()))
TN = (((0,), (0,)), ((), ()))


def dot(a, b, dims=NN):
    return lax.dot_general(a, b, dims, preferred_element_type=F32)


COST = {
    "fence": (60, 1),
    "mark": (0, 1),
    "order": (60, 8),
    "place": (1, 4),
    "bias": (60, 8),
    "qkv": (60, 12),
    "attend": (60, 12),
    "project": (60, 12),
    "ffn": (60, 15),
    "turn": (60, 12),
    "attend_back": (60, 12),
    "bucket_sums": (60, 10),
    "weights": (60, 12),
}


def call(kernel, args, out_shape, name, in_specs, out_specs, grid=(), scratch=(), deps=(), aliases=None):
    inputs = len(in_specs)
    outputs = inputs + len(deps) + len(out_shape)
    any_space = pl.BlockSpec(memory_space=pl.ANY)

    def wrapped(*refs):
        kernel(*refs[:inputs], *refs[inputs + len(deps) : outputs], *refs[outputs + 1 :])

    cost, room = COST[name]
    return pl.pallas_call(
        wrapped,
        out_shape=[*out_shape, sds((8, 128), F32)],
        grid=grid,
        in_specs=[*in_specs] + [any_space] * len(deps),
        out_specs=[*out_specs, any_space],
        scratch_shapes=scratch,
        compiler_params=pltpu.CompilerParams(vmem_limit_bytes=room * 1024 * 1024),
        input_output_aliases=aliases or {},
        cost_estimate=pl.CostEstimate(
            flops=cost * 1000000000, transcendentals=0, bytes_accessed=cost * 2000000
        ),
        name=name,
    )(*args, *deps)


def fence(*deps):
    return call(lambda: None, (), [], "fence", [], [], deps=jax.tree.leaves(deps))[0]


def mark(*deps):
    return call(lambda: None, (), [], "mark", [], [], deps=jax.tree.leaves(deps))[0]


def in_hbm(value):
    return pltpu.with_memory_space_constraint(value, pltpu.HBM)


VM = pl.BlockSpec(memory_space=pltpu.VMEM)
SM = pl.BlockSpec(memory_space=pltpu.SMEM)


def whole(*shape):
    return pl.BlockSpec(shape, lambda *_: (0,) * len(shape))


def sds(shape, dtype):
    return jax.ShapeDtypeStruct(shape, dtype)


def order_kernel(place, buckets_ref, out_ref):
    tp = place[0]
    queries, keys = buckets_ref.shape
    per = keys // 256
    for j in range(keys // 128):
        block = (place[1] ^ (j // per)) * per + (tp ^ (j % per))
        cols = pl.ds(pl.multiple_of(block * 128, 128), 128)
        for k in range(queries // 128):
            rows = pl.ds(pl.multiple_of((tp ^ k) * 128, 128), 128)
            out_ref[128 * j : 128 * j + 128, 128 * k : 128 * k + 128] = buckets_ref[rows, cols].T


def order_buckets(place, buckets, deps):
    shape = (buckets.shape[1], buckets.shape[0])
    return call(order_kernel, (place, buckets), [sds(shape, jnp.int32)], "order", [SM, VM], [VM], deps=deps)


def look_up(table_ref, head, index):
    row = jnp.broadcast_to(table_ref[pl.ds(head, 1), :], (index.shape[0], 128))
    parts = [
        jnp.take_along_axis(row, index[:, 128 * k : 128 * k + 128], axis=1, mode="promise_in_bounds")
        for k in range(index.shape[1] // 128)
    ]
    return jnp.concatenate(parts, axis=1)


def bias_kernel(half, labels, table, out_ref):
    step = pl.program_id(0)
    first = half * (labels.shape[0] // 2) + 128 * step
    index = labels[pl.ds(pl.multiple_of(first, 128), 128), :]
    rows = pl.ds(pl.multiple_of(128 * step, 128), 128)
    for h in range(out_ref.shape[0]):
        out_ref[h, rows, :] = look_up(table, h, index).astype(BF)


def position_bias(labels, table, half, deps):
    heads = table.shape[0]
    keys, queries = labels.shape
    return call(
        partial(bias_kernel, half),
        (labels, table),
        [sds((heads, keys // 2, queries), BF)],
        "bias",
        [VM, VM],
        [VM],
        grid=(keys // 256,),
        deps=deps,
    )


def qkv_kernel(place, x0, x1, x2, x3, gain, mine, other, x_out, xn_out, q_out, kv_out, a_out, o_out):
    first = place[1] == 0
    for r, ref in enumerate((x0, x1, x2, x3)):
        x = ref[...]
        x_out[128 * r : 128 * r + 128, :] = x
        xf = x.astype(F32)
        scale = lax.rsqrt(jnp.mean(xf * xf, axis=-1, keepdims=True) + EPS)
        xn_out[128 * r : 128 * r + 128, :] = (xf * scale * gain[...]).astype(BF)
    for k in range(4):
        for s in range(4):
            m = mine[place[2 + s], k]
            o = other[place[6 + s], k]
            a_out[k, 192 * s : 192 * s + 192, 0:384] = jnp.where(first, m, o)
            a_out[k, 192 * s : 192 * s + 192, 384:768] = jnp.where(first, o, m)
        for s in range(4):
            for c in range(4):
                o_out[192 * k + 48 * s : 192 * k + 48 * s + 48, 192 * c : 192 * c + 192] = a_out[
                    k, 192 * s + 48 * c : 192 * s + 48 * c + 48, 576:768
                ]
        y = dot(xn_out[...], a_out[k, :, 0:576]).astype(BF)
        q_out[:, 192 * k : 192 * k + 192] = y[:, 0:192]
        kv_out[0, :, 192 * k : 192 * k + 192] = y[:, 192:384]
        kv_out[1, :, 192 * k : 192 * k + 192] = y[:, 384:576]


def lanes_of(pair):
    return pl.ds(pl.multiple_of(128 * pair, 128), 128)


def attend_kernel(begin, q_ref, own, other, bias0, bias1, *refs):
    att_ref, full_ref, lse_ref = refs[-3:]
    pair = pl.program_id(0) + begin
    cols = lanes_of(pair)
    part_keys = own.shape[1] // 2
    qt = q_ref[:, cols].T
    vts = [own[1, :, cols].T, other[1, :, cols].T]
    side = lax.broadcasted_iota(jnp.int32, qt.shape, 0) // 64
    ones = jnp.ones((16, part_keys), BF)
    results = []
    for h in range(2):
        q = jnp.where(side == h, qt, jnp.zeros((), BF))
        scores = []
        top = None
        for i in range(4):
            rows = slice(part_keys * (i % 2), part_keys * (i % 2 + 1))
            bias = (bias0, bias1)[i // 2][2 * pair + h, rows, :]
            score = dot((own, other)[i // 2][0, rows, cols], q) + bias.astype(F32)
            high = jnp.max(score, axis=0, keepdims=True)
            top = high if i == 0 else jnp.maximum(top, high)
            scores.append(score)
        part = None
        for i, score in enumerate(scores):
            values = vts[i // 2][64 * h : 64 * h + 64, part_keys * (i % 2) : part_keys * (i % 2 + 1)]
            e = jnp.exp(score - top).astype(BF)
            piece = dot(jnp.concatenate([values, ones], axis=0), e)
            part = piece if i == 0 else part + piece
        total = part[64:65, :]
        lse_ref[pair, h : h + 1, :] = top + jnp.log(total)
        results.append(part[0:64, :] / total)
    full = jnp.concatenate(results, axis=0).T
    full_ref[:, cols] = full
    att_ref[:, cols] = full.astype(BF)


def attend(q, own, other, labels, table, begin, pairs, before, deps):
    rows, width = q.shape
    return call(
        partial(attend_kernel, begin),
        (q, own, other, labels, table, *before),
        [sds((rows, width), BF), sds((rows, width), F32), sds((width // 128, 2, rows), F32)],
        "attend",
        [VM] * (5 + len(before)),
        [VM] * 3,
        grid=(pairs,),
        deps=deps,
        aliases={5: 0, 6: 1, 7: 2} if before else None,
    )


def project_kernel(x_ref, att_ref, o_ref, gain, mid_ref, nf_ref):
    mid = x_ref[...].astype(F32) + dot(att_ref[...], o_ref[...])
    mid_ref[...] = mid
    scale = lax.rsqrt(jnp.mean(mid * mid, axis=-1, keepdims=True) + EPS)
    nf_ref[...] = (mid * scale * gain[...]).astype(BF)


def ffn_kernel(first_call, begin, place, nf_ref, g0, g1, g2, g3, mine, other, *refs):
    if first_call:
        out_ref, dnf_ref, keep, send, w1s, w2s, gs, us, ds = refs
    else:
        out_in, dnf_in = refs[:2]
        out_ref, dnf_ref, keep, send, w1s, w2s, gs, us, ds = refs[-9:]
    first = place[1] == 0
    step = pl.program_id(0)
    block = step + begin

    @pl.when(step == 0)
    def _():
        for r, ref in enumerate((g0, g1, g2, g3)):
            gs[128 * r : 128 * r + 128, :] = ref[...]
        if first_call:
            out_ref[...] = jnp.zeros_like(out_ref)
            dnf_ref[...] = jnp.zeros_like(dnf_ref)
        else:
            out_ref[...] = out_in[...]
            dnf_ref[...] = dnf_in[...]

    for s in range(4):
        rows = slice(192 * s, 192 * s + 192)
        for i, w in enumerate((w1s, w2s)):
            m = mine[place[2 + s], block, i]
            o = other[place[6 + s], block, i]
            w[rows, 0:384] = jnp.where(first, m, o)
            w[rows, 384:768] = jnp.where(first, o, m)
    for j in range(3):
        cols = slice(256 * j, 256 * j + 256)
        v = dot(nf_ref[...], w1s[:, cols])
        square = v * v
        th = jnp.tanh(v * (0.7978845608 + (0.7978845608 * 0.044715) * square))
        half = 0.5 + 0.5 * th
        us[:, cols] = (v * half).astype(BF)
        slope = half + v * (0.5 - 0.5 * th * th) * (0.7978845608 + (0.7978845608 * 3 * 0.044715) * square)
        ds[:, cols] = (dot(gs[...], w2s[cols, :], NT) * slope).astype(BF)
    out_ref[...] += dot(us[...], w2s[...])
    dnf_ref[...] += dot(ds[...], w1s[...], NT)
    d1 = dot(nf_ref[...], ds[...], TN).astype(BF)
    d2 = dot(us[...], gs[...], TN).astype(BF)
    for s in range(4):
        rows = slice(192 * s, 192 * s + 192)
        for i, d in enumerate((d1, d2)):
            lo = d[rows, 0:384]
            hi = d[rows, 384:768]
            keep[place[2 + s], block, i] = jnp.where(first, lo, hi)
            send[place[6 + s], block, i] = jnp.where(first, hi, lo)


def ffn_blocks(place, nf, g, mine, other, carry, grads, begin, count, deps):
    rows, width = nf.shape
    aliases = {}
    if carry:
        aliases = {8: 0, 9: 1}
    if grads:
        aliases.update({10: 2, 11: 3})
    return call(
        partial(ffn_kernel, not carry, begin),
        (place, nf, *g, mine, other, *carry, *grads),
        [sds((rows, width), F32), sds((rows, width), F32)] + [sds(mine.shape, BF)] * 2,
        "ffn",
        [SM] + [VM] * (7 + len(carry) + len(grads)),
        [VM] * 4,
        grid=(count,),
        scratch=[pltpu.VMEM((width, width), BF)] * 2 + [pltpu.VMEM((rows, width), BF)] * 3,
        deps=deps,
        aliases=aliases,
    )


def store_gain(ref, value):
    for i in range(ref.shape[0]):
        ref[i : i + 1, :] = value[:, 128 * i : 128 * i + 128]


def turn_kernel(mid_ref, out_in, dnf_in, g0, g1, g2, g3, gain, o_ref, full_ref, h0, h1, h2, h3, dmid_ref, dml_ref, da_ref, delta_ref, gg_ref):
    mid = mid_ref[...]
    hid = (mid + out_in[...]).astype(BF)
    for r, ref in enumerate((h0, h1, h2, h3)):
        ref[...] = hid[128 * r : 128 * r + 128, :]
    scale = lax.rsqrt(jnp.mean(mid * mid, axis=-1, keepdims=True) + EPS)
    up = dnf_in[...]
    weighted = up * gain[...]
    mean_term = jnp.mean(weighted * mid, axis=-1, keepdims=True)
    res = scale * weighted - mid * (scale * scale * scale) * mean_term
    store_gain(gg_ref, jnp.sum(up * mid * scale, axis=0, keepdims=True))
    for r, ref in enumerate((g0, g1, g2, g3)):
        rows = slice(128 * r, 128 * r + 128)
        dmid_ref[rows, :] = res[rows, :] + ref[...].astype(F32)
    low = dmid_ref[...].astype(BF)
    dml_ref[...] = low
    da = dot(low, o_ref[...], NT).astype(BF)
    da_ref[...] = da
    pairs = delta_ref.shape[0]
    width = da.shape[1]
    head = lax.broadcasted_iota(jnp.int32, (2 * pairs, width), 0)
    lane = lax.broadcasted_iota(jnp.int32, (2 * pairs, width), 1)
    pick = jnp.where(lane // 64 == head, 1.0, 0.0)
    delta = lax.dot_general(
        pick, da.astype(F32) * full_ref[...], NT, precision=lax.Precision.HIGHEST, preferred_element_type=F32
    )
    for p in range(pairs):
        delta_ref[p] = delta[2 * p : 2 * p + 2, :]


def split_rows(value):
    row = lax.broadcasted_iota(jnp.int32, (64, value.shape[1]), 0)
    out = jnp.zeros((64, value.shape[1]), BF)
    for i in range(3):
        piece = value.astype(BF)
        out = jnp.where(row == i, piece, out)
        value = value - piece.astype(F32)
    return out


def attend_back_kernel(begin, half, last, q_ref, da_ref, kv_ref, labels, table, lse_ref, delta_ref, *refs):
    if last:
        dq_in, dq_ref, dkv_ref, ds_ref = refs
    else:
        dq_ref, dkv_ref, ds_ref = refs
    pair = pl.program_id(0) + begin
    cols = lanes_of(pair)
    outs = lanes_of(pl.program_id(0))
    part_keys = kv_ref.shape[1] // 2
    zero = jnp.zeros((), BF)
    q_all, da_all = q_ref[:, cols], da_ref[:, cols]
    qt = q_all.T
    dat = da_all.T
    kt = kv_ref[0, :, cols].T
    lane = lax.broadcasted_iota(jnp.int32, (1, 128), 1)
    dqs = [None, None]
    qs, das, qas, daas = [], [], [], []
    for h in range(2):
        own = lane // 64 == h
        qs.append(jnp.where(own, q_all, zero))
        das.append(jnp.where(own, da_all, zero))
        for t, stat, out in ((qt, lse_ref, qas), (dat, delta_ref, daas)):
            extra = split_rows(stat[pair, h : h + 1, :])
            mine = t[64 * h : 64 * h + 64, :]
            out.append(jnp.concatenate([mine, extra] if h == 0 else [extra, mine], axis=0))
    for i in range(2):
        rows = slice(part_keys * i, part_keys * (i + 1))
        k = kv_ref[0, rows, cols]
        v = kv_ref[1, rows, cols]
        dk = dv = None
        for h in range(2):
            own = lane // 64 == h
            minus = jnp.where(lane % 64 < 3, -1.0, 0.0).astype(BF)
            first = half * kv_ref.shape[1] + part_keys * i
            bias = look_up(table, 2 * pair + h, labels[first : first + part_keys, :])
            p = jnp.exp(dot(jnp.where(own, k, minus), qas[h]) + bias)
            ds = (p * dot(jnp.where(own, v, minus), daas[h])).astype(BF)
            ds_ref[2 * pl.program_id(0) + h, rows, :] = ds
            a = dot(kt[64 * h : 64 * h + 64, rows], ds)
            b = dot(ds, qs[h])
            c = dot(p.astype(BF), das[h])
            dqs[h] = a if i == 0 else dqs[h] + a
            dk, dv = (b, c) if h == 0 else (dk + b, dv + c)
        dkv_ref[0, rows, outs] = dk.astype(dkv_ref.dtype)
        dkv_ref[1, rows, outs] = dv.astype(dkv_ref.dtype)
    dq = jnp.concatenate(dqs, axis=0).T
    if last:
        dq_ref[:, outs] = (dq_in[:, outs] + dq).astype(dq_ref.dtype)
    else:
        dq_ref[:, outs] = dq


def attend_back(q, da, kv, labels, table, half, begin, pairs, lse, delta, dq, deps):
    rows = q.shape[0]
    width = 128 * pairs
    keys = kv.shape[1]
    last = len(dq) > 0
    return call(
        partial(attend_back_kernel, begin, half, last),
        (q, da, kv, labels, table, lse, delta, *dq),
        [
            sds((rows, width), BF if last else F32),
            sds((2, keys, width), F32 if last else BF),
            sds((2 * pairs, keys, rows), BF),
        ],
        "attend_back",
        [VM] * (7 + len(dq)),
        [VM] * 3,
        grid=(pairs,),
        deps=deps,
    )


def weights_kernel(blocks, last, place, xn_ref, dq_ref, dkv_in, dkv_add, a_ref, att_ref, dml_ref, *refs):
    if last:
        up_in, dmid_ref, x_ref, gain, keep, send, h0, h1, h2, h3, gg_ref = refs
        up = up_in[...]
    else:
        keep, send, up_ref = refs
        up = None
    first = place[1] == 0
    dq = dq_ref[...]
    dk, dv = ((dkv_in[i] + dkv_add[i].astype(F32)).astype(BF) for i in range(2))
    xn = xn_ref[...]
    for i, k in enumerate(blocks):
        cols = slice(192 * i, 192 * i + 192)
        cat = jnp.concatenate([dq[:, cols], dk[:, cols], dv[:, cols]], axis=1)
        part = dot(cat, a_ref[k, :, 0:576], NT)
        up = part if up is None else up + part
        grad = dot(xn, cat, TN).astype(BF)
        out = dot(att_ref[:, 192 * k : 192 * k + 192], dml_ref[...], TN).astype(BF)
        for s in range(4):
            rows = slice(192 * s, 192 * s + 192)
            lo = grad[rows, 0:384]
            piece = jnp.concatenate(
                [out[48 * s : 48 * s + 48, 192 * c : 192 * c + 192] for c in range(4)], axis=0
            )
            hi = jnp.concatenate([grad[rows, 384:576], piece], axis=1)
            keep[place[2 + s], i] = jnp.where(first, lo, hi)
            send[place[6 + s], i] = jnp.where(first, hi, lo)
    if not last:
        up_ref[...] = up
        return
    x = x_ref[...].astype(F32)
    scale = lax.rsqrt(jnp.mean(x * x, axis=-1, keepdims=True) + EPS)
    weighted = up * gain[...]
    mean_term = jnp.mean(weighted * x, axis=-1, keepdims=True)
    res = scale * weighted - x * (scale * scale * scale) * mean_term
    store_gain(gg_ref, jnp.sum(up * x * scale, axis=0, keepdims=True))
    back = (dmid_ref[...] + res).astype(BF)
    for r, ref in enumerate((h0, h1, h2, h3)):
        ref[...] = back[128 * r : 128 * r + 128, :]


def place_kernel(place, mine, other, q_out, k_out, v_out, o_out):
    first = place[1] == 0
    lo = jnp.where(first, mine[...], other[...]).astype(F32)
    hi = jnp.where(first, other[...], mine[...]).astype(F32)
    q_out[...] = lo[:, 0:192]
    k_out[...] = lo[:, 192:384]
    v_out[...] = hi[:, 0:192]
    for i in range(4):
        o_out[:, 192 * i : 192 * i + 192] = hi[48 * i : 48 * i + 48, 192:384]


def bucket_kernel(source, adds, place, labels, ds0_ref, ds1_ref, *refs):
    before = refs[0] if adds else None
    out_ref, acc, table = refs[-3:]
    tp = place[0]
    step = pl.program_id(0)
    heads, _, queries = ds0_ref.shape
    group = 128
    first = source * (labels.shape[0] // 2) + step * group

    @pl.when(step == 0)
    def _():
        acc[...] = jnp.zeros_like(acc)

    label = [(lax.broadcasted_iota(jnp.int32, (16, 128), 0) + 16 * i).astype(F32).astype(BF) for i in range(2)]
    one, zero = jnp.ones((), BF), jnp.zeros((), BF)
    for g in range(group // 16):
        for k in range(queries // 128):
            index = labels[pl.ds(pl.multiple_of(first + 16 * g, 16), 16), 128 * k : 128 * k + 128].astype(F32)
            for j in range(16):
                spread = jnp.broadcast_to(index[j : j + 1, :], (16, 128)).astype(BF)
                for i in range(2):
                    at = 32 * j + 16 * i
                    table[at : at + 16, 128 * k : 128 * k + 128] = jnp.where(spread == label[i], one, zero)
        part = pl.ds(pl.multiple_of(step * group + 16 * g, 16), 16)
        left = [d[:, part, :].reshape(heads * 16, queries) for d in (ds0_ref, ds1_ref)]
        acc[...] += dot(jnp.concatenate(left, axis=0), table[...], NT)

    @pl.when(step == pl.num_programs(0) - 1)
    def _():
        row = lax.broadcasted_iota(jnp.int32, acc.shape, 0) % 16
        col = lax.broadcasted_iota(jnp.int32, acc.shape, 1) // 32
        hit = jnp.where(row == col, acc[...], 0.0)
        fold = (hit[:, 0:128] + hit[:, 128:256]) + (hit[:, 256:384] + hit[:, 384:512])
        sums = jnp.sum(fold.reshape(2 * heads, 16, 128), axis=1)
        sums = sums + pltpu.roll(sums, 64, 1)
        sums = sums + pltpu.roll(sums, 32, 1)
        lane = lax.broadcasted_iota(jnp.int32, sums.shape, 1)
        sums = jnp.where(lane < 32, sums, 0.0)
        out_ref[...] = jnp.zeros_like(out_ref) if before is None else before[...]
        each = heads // 2
        for k in range(4):
            for h in range(each):
                at = (tp ^ ORDER[k]) * each + h
                out_ref[pl.ds(at, 1), :] = out_ref[pl.ds(at, 1), :] + sums[each * k + h : each * k + h + 1, :]


def bucket_sums(place, half, labels, ds, before, deps):
    heads, keys, queries = ds[0].shape
    return call(
        partial(bucket_kernel, half, len(before)),
        (place, labels, ds[0], ds[1], *before),
        [sds((16, 128), F32)],
        "bucket_sums",
        [SM] + [VM] * (3 + len(before)),
        [VM],
        grid=(keys // 128,),
        scratch=[pltpu.VMEM((heads * 32, 512), F32), pltpu.VMEM((512, queries), BF)],
        deps=deps,
    )


def move(value, move_to, sizes):
    shards, ctx, tps = sizes
    pairs = []
    for s in range(shards):
        for c in range(ctx):
            for t in range(tps):
                a, b, d = move_to(s, c, t)
                pairs.append(((s * ctx + c) * tps + t, (a * ctx + b) * tps + d))
    return lax.ppermute(value, ALL, pairs)


def body(
    hidden_in,
    norm_attn_gain,
    query_weight,
    key_weight,
    value_weight,
    out_weight,
    bias_table,
    norm_ffn_gain,
    ffn_in_weight,
    ffn_out_weight,
    buckets,
    output_gradient,
):
    sizes = tuple(lax.axis_size(a) for a in ALL)
    shards, ctxs, tps = sizes
    s, c, t = (lax.axis_index(a) for a in ALL)
    fast = shards == 4
    assert ctxs == 2 and tps == 4 and hidden_in.shape[0] == tps
    heads = bias_table.shape[1]

    def along(k):
        return lambda a, b, d: (a, b, d ^ k)

    def across(a, b, d):
        return (a, 1 - b, d)

    def near(a, b, d):
        return (a ^ (1 if b == 0 else 2), b, d)

    def far(a, b, d):
        return (a ^ (2 if b == 0 else 1), b, d)

    go = partial(move, sizes=sizes)

    def spot(shard, core):
        d = shard ^ s
        return jnp.where(core == 0, d, (d >> 1) | ((d & 1) << 1)) if fast else jnp.int32(shard)

    place = jnp.stack(
        [t, c] + [spot(i, c) for i in range(4)] + [spot(i, 1 - c) for i in range(4)]
    ).astype(jnp.int32)

    def pick(value, k):
        return lax.dynamic_index_in_dim(value, t ^ k, 0, keepdims=False)

    def tie(value, token):
        return lax.optimization_barrier((value, token))

    def add(a, b):
        return (a.astype(F32) + b.astype(F32)).astype(BF)

    def send_near(value):
        return go(value, near) if fast else value

    def send_far(value):
        return go(value, far) if fast else value

    def join_near(value, got):
        return jnp.stack([value, got]) if fast else value

    def join_far(value, got):
        if fast:
            return jnp.concatenate([value, got])
        full = lax.all_gather(value, "shard", axis=0, tiled=False)
        full = jnp.moveaxis(full, 0, -3)
        lead = full.shape[:-3]
        return jnp.moveaxis(full.reshape(lead + (4, 192, 384)), -3, 0)

    def stage_far(keep, got):
        if fast:
            return add(keep[:2], got[:2]), add(keep[2:], got[2:])
        return add(keep, got), jnp.zeros((8, 128), BF)

    def stage_near(stay, got):
        return (add(stay[0], got[0]), add(stay[1], got[1])) if fast else (stay, got)

    def stage_last(stay, got):
        if fast:
            return [add(stay[i], got[i]) for i in range(stay.shape[0])]
        total = jnp.moveaxis(stay, 0, -3)
        lead = total.shape[:-3]
        total = jnp.moveaxis(total.reshape(lead + (shards, 768 // shards, 384)), -3, 0)
        total = lax.psum_scatter(total, "shard", scatter_dimension=0, tiled=False)
        return [total[i] for i in range(total.shape[0])]

    def my_half(lo, hi):
        return jnp.where(c == 0, lo, hi)

    def both_halves(mine, other):
        return jnp.where(c == 0, mine, other).astype(F32), jnp.where(c == 0, other, mine).astype(F32)

    width = hidden_in.shape[2]
    n = 512
    ga = norm_attn_gain.reshape(1, width)
    gf = norm_ffn_gain.reshape(1, width)
    row = sds((n, width), BF)
    out_rows = out_weight.shape[0]

    out_pack = jnp.concatenate([out_weight[:, 192 * i : 192 * i + 192] for i in range(4)], axis=0)
    att_half = my_half(
        jnp.concatenate([query_weight, key_weight], axis=1), jnp.concatenate([value_weight, out_pack], axis=1)
    )
    ffn_half = my_half(
        jnp.stack([ffn_in_weight[:, :384], ffn_out_weight[:, :384]]),
        jnp.stack([ffn_in_weight[:, 384:], ffn_out_weight[:, 384:]]),
    )
    head_order = jnp.concatenate([(t ^ k) * (heads // tps) + jnp.arange(heads // tps) for k in ORDER])
    table_rel = jnp.pad(jnp.take(bias_table.T, head_order, axis=0), ((0, 0), (0, 128 - bias_table.shape[0])))

    def both(value, token):
        return lax.optimization_barrier((value, token))

    pair = jnp.stack([att_half, go(att_half, along(2))])
    a0 = go(pair, along(1))
    own = send_near(ffn_half)
    own, pair = both(own, pair)
    own = join_near(ffn_half, own)
    own_m = send_far(own)
    xs = [pick(hidden_in, k) for k in range(tps)]
    labels, tok = order_buckets(place, buckets, [pair, own, *xs])
    (a0, own_m), tok = tie((a0, own_m), tok)
    own_m = join_far(own, own_m)
    a0 = jnp.concatenate([pair, a0])
    a1 = send_near(a0)
    xs, a0 = both(xs, a0)
    zx = [go(xs[k], along(k)) for k in (1, 2, 3)]
    tok = fence(tok, a0, *xs)
    a1, tok = tie(a1, tok)
    a1 = join_near(a0, a1)
    am = send_far(a1)
    bias = [None] * 2
    bias[0], tok = position_bias(labels, table_rel, 0, [tok, a1])
    zx, tok = tie(zx, tok)
    ffn_w, zx = both(ffn_half, zx)
    w2 = go(ffn_w, along(2))
    tok = mark(tok, ffn_w)
    am, tok = tie(am, tok)
    am = join_far(a1, am)
    ao = go(am, across)
    bias[1], tok = position_bias(labels, table_rel, 1, [tok, am])
    ao, tok = tie(ao, tok)
    x_parts = [xs[0]] + zx
    if not fast:
        def regroup(z):
            part = z[..., 192:].reshape(4, 4, shards // 4, 4, out_rows, 192)
            part = jnp.transpose(part, (0, 1, 3, 2, 4, 5)).reshape(4, 4, 192, 192)
            return jnp.concatenate([z[..., :192], part], axis=-1)

        fixed_m, fixed_o = regroup(am), regroup(ao)
        am, ao = jnp.where(c == 1, fixed_m, am), jnp.where(c == 0, fixed_o, ao)

    x, xn, q, kv, a_full, o_full, tok = call(
        qkv_kernel,
        (place, *x_parts, ga, am, ao),
        [row, row, row, sds((2, n, width), BF), sds((4, width, width), BF), sds((width, width), BF)],
        "qkv",
        [SM] + [VM] * 7,
        [VM] * 6,
        deps=[tok],
    )
    kv_other = go(kv, across)
    tok = mark(tok, kv)
    w2, tok = tie(w2, tok)
    pair_w = jnp.stack([ffn_half, w2])
    pb = go(pair_w, along(1))
    w2, pair_w = both(w2, pair_w)
    pan = send_near(w2)
    tok = fence(tok, pair_w, w2)
    kv_other, tok = tie(kv_other, tok)
    att, full, lse, tok = attend(q, kv, kv_other, *bias, 0, 3, (), [tok])
    (pan, pb), tok = tie((pan, pb), tok)
    pa = join_near(w2, pan)
    pam = send_far(pa)
    pbn = send_near(pb)
    gs, pb = both([pick(output_gradient, kk) for kk in range(tps)], pb)
    zg = {kk: go(gs[kk], along(kk)) for kk in (1, 2, 3)}
    att, full, lse, tok = attend(q, kv, kv_other, *bias, 3, 3, (att, full, lse), [tok, pa, pb, *gs])
    (pam, pbn), tok = tie((pam, pbn), tok)
    pam = jnp.stack([own_m, join_far(pa, pam)], axis=1)
    pao = go(pam, across)
    pb = join_near(pb, pbn)
    pbm = send_far(pb)
    mid, nf, tok = call(
        project_kernel,
        (x, att, o_full, gf),
        [sds((n, width), F32), row],
        "project",
        [VM] * 4,
        [VM] * 2,
        deps=[tok, pam, pb],
    )
    (zg, pao), tok = tie((zg, pao), tok)
    g_parts = [gs[0]] + [zg[kk] for kk in (1, 2, 3)]

    out_acc, dnf, keep_a, send_a, tok = ffn_blocks(place, nf, g_parts, pam, pao, (), (), 0, 2, [tok])
    cross_a = go(send_a, across)
    pbm, tok = tie(pbm, tok)
    pbm = join_far(pb, pbm)
    pbo = go(pbm, across)
    tok = fence(tok, pbm, send_a)
    pbo, tok = tie(pbo, tok)
    out_acc, dnf, keep_b, send_b, tok = ffn_blocks(
        place, nf, g_parts, pbm, pbo, (out_acc, dnf), (), 0, 1, [tok, send_a]
    )
    cross_a, tok = tie(cross_a, tok)
    stay_a, leave_a = stage_far(keep_a, cross_a)
    far_a = send_far(leave_a)
    out_acc, dnf, keep_b, send_b, tok = ffn_blocks(
        place, nf, g_parts, pbm, pbo, (out_acc, dnf), (keep_b, send_b), 1, 1, [tok, stay_a, leave_a]
    )
    cross_b = go(send_b, across)

    piece = sds((n // tps, width), BF)
    gain_rows = sds((width // 128, 128), F32)
    *hids, dmid, dml, da, delta, gf_grad, tok = call(
        turn_kernel,
        (mid, out_acc, dnf, *g_parts, gf, o_full, full),
        [piece] * 4 + [sds((n, width), F32), row, row, sds((heads // 2, 2, n), F32), gain_rows],
        "turn",
        [VM] * 10,
        [VM] * 9,
        deps=[tok, send_b],
    )

    def arrange(pieces):
        stacked = jnp.stack(pieces)
        return jnp.stack([pick(stacked, i) for i in range(tps)])

    hid_parts = [go(hids[k], along(k)) for k in (1, 2, 3)]
    (cross_b, far_a), tok = tie((cross_b, far_a), tok)
    stay_a, leave_a = stage_near(stay_a, far_a)
    near_a = send_near(leave_a)
    stay_b, leave_b = stage_far(keep_b, cross_b)
    far_b = send_far(leave_b)
    dq1, dkv1, ds11, tok = attend_back(
        q, da, kv_other, labels, table_rel, 1, 3, 3, lse, delta, (), [tok, stay_b, leave_b, stay_a, leave_a, *hids]
    )
    dkv1 = go(dkv1, across)
    first_hids, tok = tie(hid_parts[:2], tok)
    hid_parts = [*first_hids, hid_parts[2]]
    dq1, own1, ds01, tok = attend_back(
        q, da, kv, labels, table_rel, 0, 3, 3, lse, delta, (dq1,), [tok]
    )
    (near_a, far_b, dkv1, hid_parts[2]), tok = tie((near_a, far_b, dkv1, hid_parts[2]), tok)
    blocks_a = stage_last(stay_a, near_a)
    stay_b, leave_b = stage_near(stay_b, far_b)
    near_b = send_near(leave_b)

    keep_v, send_v, up, tok = call(
        partial(weights_kernel, (2, 3), False),
        (place, xn, dq1, own1, dkv1, a_full, att, dml),
        [sds((4, 2, 192, 384), BF), sds((4, 2, 192, 384), BF), sds((n, width), F32)],
        "weights",
        [SM] + [VM] * 7,
        [VM] * 3,
        deps=[tok, stay_b, leave_b, *blocks_a, *hid_parts],
    )
    if not fast:
        def ungroup(z):
            part = z[..., 192:].reshape(4, 2, 4, shards // 4, out_rows, 192)
            part = jnp.transpose(part, (0, 1, 3, 2, 4, 5)).reshape(4, 2, 192, 192)
            return jnp.concatenate([z[..., :192], part], axis=-1)

        def ungroup_both(keep, send):
            return jnp.where(c == 1, ungroup(keep), keep), jnp.where(c == 0, ungroup(send), send)

        keep_v, send_v = ungroup_both(keep_v, send_v)
    cross_v = go(send_v, across)
    near_b, tok = tie(near_b, tok)
    blocks_b = jnp.stack(stage_last(stay_b, near_b))
    zb = go(blocks_b, along(1))
    dq0, dkv0, ds10, tok = attend_back(
        q, da, kv_other, labels, table_rel, 1, 0, 3, lse, delta, (), [tok, send_v, blocks_b]
    )
    dkv0 = go(dkv0, across)
    cross_v, tok = tie(cross_v, tok)
    stay_v, leave_v = stage_far(keep_v, cross_v)
    far_v = send_far(leave_v)
    dq0, own0, ds00, tok = attend_back(
        q, da, kv, labels, table_rel, 0, 0, 3, lse, delta, (dq0,), [tok, stay_v, leave_v]
    )
    (far_v, dkv0, zb), tok = tie((far_v, dkv0, zb), tok)
    c0, c2 = add(blocks_a[0], zb[0]), add(blocks_a[1], zb[1])
    zc = go(c2, along(2))
    stay_v, leave_v = stage_near(stay_v, far_v)
    near_v = send_near(leave_v)
    sums, tok = bucket_sums(place, 1, labels, (ds10, ds11), (), [tok, stay_v, leave_v, dkv0, c0, c2])
    near_v, tok = tie(near_v, tok)
    blocks_v = jnp.stack(stage_last(stay_v, near_v))
    zv = go(blocks_v, along(1))
    keep_w, send_w, *backs, ga_grad, tok = call(
        partial(weights_kernel, (0, 1), True),
        (place, xn, dq0, own0, dkv0, a_full, att, dml, up, dmid, x, ga),
        [sds((4, 2, 192, 384), BF)] * 2 + [piece] * 4 + [gain_rows],
        "weights",
        [SM] + [VM] * 11,
        [VM] * 7,
        deps=[tok, blocks_v],
    )
    if not fast:
        keep_w, send_w = ungroup_both(keep_w, send_w)
    cross_w = go(send_w, across)
    zc, tok = tie(zc, tok)
    ffn_mine = add(c0, zc)
    back_parts = [backs[0]] + [go(backs[k], along(k)) for k in (1, 2)]
    tok = fence(tok, backs, send_w, ffn_mine)
    cross_w, tok = tie(cross_w, tok)
    stay_w, leave_w = stage_far(keep_w, cross_w)
    far_w = send_far(leave_w)
    sums, tok = bucket_sums(place, 0, labels, (ds00, ds01), (sums,), [tok, stay_w, leave_w])
    (far_w, zv, got_backs), tok = tie((far_w, zv, back_parts), tok)
    ffn_mine, zv = both(ffn_mine, zv)
    ffn_other = go(ffn_mine, across)
    stay_w, leave_w = stage_near(stay_w, far_w)
    near_w = send_near(leave_w)
    back3 = go(backs[3], along(3))
    small = jnp.concatenate([sums, jnp.pad(ga_grad, ((0, 2), (0, 0))), jnp.pad(gf_grad, ((0, 2), (0, 0)))])
    got = go(small, across)
    tok = fence(tok, stay_w, leave_w, small, ffn_mine)
    (got, ffn_other), tok = tie((got, ffn_other), tok)
    small = small + got
    ffn_lo, ffn_hi = both_halves(ffn_mine, ffn_other)
    if fast:
        got = go(small, lambda a, b, d: (a ^ 1, b, d))
        tok = fence(tok, small)
        (got, near_w), tok = tie((got, near_w), tok)
        small = small + got
        got = go(small, lambda a, b, d: (a ^ 2, b, d))
    else:
        small = lax.psum(small, "shard")
    blocks_w = stage_last(stay_w, near_w)
    d0, d2 = add(blocks_w[0], zv[0]), add(blocks_w[1], zv[1])
    zw = go(d2, along(2))
    w1_grad = jnp.concatenate([ffn_lo[0], ffn_hi[0]], axis=1)
    w2_grad = jnp.concatenate([ffn_lo[1], ffn_hi[1]], axis=1)
    tok = fence(tok, small, d0, d2, w1_grad, w2_grad)
    if fast:
        got, tok = tie(got, tok)
        small = small + got
    got = go(small, along(1))
    tok = fence(tok, small)
    (got, zw, back3), tok = tie((got, zw, back3), tok)
    small = small + got
    got = go(small, along(2))
    att_mine = add(d0, zw)
    att_other = go(att_mine, across)
    hidden_grad = arrange([*got_backs, back3]).astype(F32)
    tok = fence(tok, small, att_mine, hidden_grad)
    (got, att_other), tok = tie((got, att_other), tok)
    small = small + got
    hidden_out = arrange([hids[0]] + hid_parts)
    table_grad = small[:heads, : bias_table.shape[0]].T
    gains = width // 128

    if fast:
        part = sds((192, 192), F32)
        q_grad, k_grad, v_grad, out_grad, _ = call(
            place_kernel,
            (place, att_mine, att_other),
            [part, part, part, sds((out_rows, width), F32)],
            "place",
            [SM, VM, VM],
            [VM] * 4,
        )
    else:
        att_lo, att_hi = both_halves(att_mine, att_other)
        q_grad, k_grad, v_grad = att_lo[:, :192], att_lo[:, 192:], att_hi[:, :192]
        out_grad = jnp.concatenate([att_hi[out_rows * i : out_rows * i + out_rows, 192:] for i in range(4)], axis=1)
    return (
        hidden_out,
        hidden_grad,
        small[16 : 16 + gains].reshape(width),
        q_grad,
        k_grad,
        v_grad,
        out_grad,
        table_grad,
        small[24 : 24 + gains].reshape(width),
        w1_grad,
        w2_grad,
    )


def solution(mesh):
    rows = P("shard", ("ctx", "tp"), None)
    cols = P("shard", "tp")
    both = P(("tp", "shard"), None)
    return jax.shard_map(
        body,
        mesh=mesh,
        in_specs=(rows, P(), cols, cols, cols, both, P(), P(), cols, both, P("ctx", None), rows),
        out_specs=(rows, rows, P(), cols, cols, cols, both, P(), P(), cols, both),
        check_vma=False,
    )
```

```python
from functools import partial

import jax
import jax.numpy as jnp
from jax import lax
from jax.experimental import pallas as pl
from jax.experimental.pallas import tpu as pltpu
from jax.sharding import PartitionSpec as P

EPS = 1e-06
F32 = jnp.float32
BF = jnp.bfloat16
ALL = ("shard", "ctx", "tp")
ORDER = (0, 2, 1, 3)
NN = (((1,), (0,)), ((), ()))
NT = (((1,), (1,)), ((), ()))
TN = (((0,), (0,)), ((), ()))


def dot(a, b, dims=NN):
    return lax.dot_general(a, b, dims, preferred_element_type=F32)


COST = {
    "fence": (60, 1),
    "mark": (0, 1),
    "order": (60, 8),
    "place": (1, 4),
    "bias": (60, 8),
    "qkv": (60, 12),
    "attend": (60, 12),
    "project": (60, 12),
    "ffn": (60, 15),
    "turn": (60, 12),
    "attend_back": (60, 12),
    "bucket_sums": (60, 10),
    "weights": (60, 12),
}


def call(kernel, args, out_shape, name, in_specs, out_specs, grid=(), scratch=(), deps=(), aliases=None):
    inputs = len(in_specs)
    outputs = inputs + len(deps) + len(out_shape)
    any_space = pl.BlockSpec(memory_space=pl.ANY)

    def wrapped(*refs):
        kernel(*refs[:inputs], *refs[inputs + len(deps) : outputs], *refs[outputs + 1 :])

    cost, room = COST[name]
    return pl.pallas_call(
        wrapped,
        out_shape=[*out_shape, sds((8, 128), F32)],
        grid=grid,
        in_specs=[*in_specs] + [any_space] * len(deps),
        out_specs=[*out_specs, any_space],
        scratch_shapes=scratch,
        compiler_params=pltpu.CompilerParams(vmem_limit_bytes=room * 1024 * 1024),
        input_output_aliases=aliases or {},
        cost_estimate=pl.CostEstimate(
            flops=cost * 1000000000, transcendentals=0, bytes_accessed=cost * 2000000
        ),
        name=name,
    )(*args, *deps)


def fence(*deps):
    return call(lambda: None, (), [], "fence", [], [], deps=jax.tree.leaves(deps))[0]


def mark(*deps):
    return call(lambda: None, (), [], "mark", [], [], deps=jax.tree.leaves(deps))[0]


def in_hbm(value):
    return pltpu.with_memory_space_constraint(value, pltpu.HBM)


VM = pl.BlockSpec(memory_space=pltpu.VMEM)
SM = pl.BlockSpec(memory_space=pltpu.SMEM)


def whole(*shape):
    return pl.BlockSpec(shape, lambda *_: (0,) * len(shape))


def sds(shape, dtype):
    return jax.ShapeDtypeStruct(shape, dtype)


def order_kernel(place, buckets_ref, out_ref):
    tp = place[0]
    queries, keys = buckets_ref.shape
    per = keys // 256
    for j in range(keys // 128):
        block = (place[1] ^ (j // per)) * per + (tp ^ (j % per))
        cols = pl.ds(pl.multiple_of(block * 128, 128), 128)
        for k in range(queries // 128):
            rows = pl.ds(pl.multiple_of((tp ^ k) * 128, 128), 128)
            out_ref[128 * j : 128 * j + 128, 128 * k : 128 * k + 128] = buckets_ref[rows, cols].T


def order_buckets(place, buckets, deps):
    shape = (buckets.shape[1], buckets.shape[0])
    return call(order_kernel, (place, buckets), [sds(shape, jnp.int32)], "order", [SM, VM], [VM], deps=deps)


def look_up(table_ref, head, index):
    row = jnp.broadcast_to(table_ref[pl.ds(head, 1), :], (index.shape[0], 128))
    parts = [
        jnp.take_along_axis(row, index[:, 128 * k : 128 * k + 128], axis=1, mode="promise_in_bounds")
        for k in range(index.shape[1] // 128)
    ]
    return jnp.concatenate(parts, axis=1)


def bias_kernel(half, labels, table, out_ref):
    step = pl.program_id(0)
    first = half * (labels.shape[0] // 2) + 128 * step
    index = labels[pl.ds(pl.multiple_of(first, 128), 128), :]
    rows = pl.ds(pl.multiple_of(128 * step, 128), 128)
    for h in range(out_ref.shape[0]):
        out_ref[h, rows, :] = look_up(table, h, index).astype(BF)


def position_bias(labels, table, half, deps):
    heads = table.shape[0]
    keys, queries = labels.shape
    return call(
        partial(bias_kernel, half),
        (labels, table),
        [sds((heads, keys // 2, queries), BF)],
        "bias",
        [VM, VM],
        [VM],
        grid=(keys // 256,),
        deps=deps,
    )


def qkv_kernel(place, x0, x1, x2, x3, gain, mine, other, x_out, xn_out, q_out, kv_out, a_out, o_out):
    first = place[1] == 0
    for r, ref in enumerate((x0, x1, x2, x3)):
        x = ref[...]
        x_out[128 * r : 128 * r + 128, :] = x
        xf = x.astype(F32)
        scale = lax.rsqrt(jnp.mean(xf * xf, axis=-1, keepdims=True) + EPS)
        xn_out[128 * r : 128 * r + 128, :] = (xf * scale * gain[...]).astype(BF)
    for k in range(4):
        for s in range(4):
            m = mine[place[2 + s], k]
            o = other[place[6 + s], k]
            a_out[k, 192 * s : 192 * s + 192, 0:384] = jnp.where(first, m, o)
            a_out[k, 192 * s : 192 * s + 192, 384:768] = jnp.where(first, o, m)
        for s in range(4):
            for c in range(4):
                o_out[192 * k + 48 * s : 192 * k + 48 * s + 48, 192 * c : 192 * c + 192] = a_out[
                    k, 192 * s + 48 * c : 192 * s + 48 * c + 48, 576:768
                ]
        y = dot(xn_out[...], a_out[k, :, 0:576]).astype(BF)
        q_out[:, 192 * k : 192 * k + 192] = y[:, 0:192]
        kv_out[0, :, 192 * k : 192 * k + 192] = y[:, 192:384]
        kv_out[1, :, 192 * k : 192 * k + 192] = y[:, 384:576]


def lanes_of(pair):
    return pl.ds(pl.multiple_of(128 * pair, 128), 128)


def attend_kernel(begin, q_ref, own, other, bias0, bias1, *refs):
    att_ref, full_ref, lse_ref = refs[-3:]
    pair = pl.program_id(0) + begin
    cols = lanes_of(pair)
    part_keys = own.shape[1] // 2
    qt = q_ref[:, cols].T
    vts = [own[1, :, cols].T, other[1, :, cols].T]
    side = lax.broadcasted_iota(jnp.int32, qt.shape, 0) // 64
    ones = jnp.ones((16, part_keys), BF)
    results = []
    for h in range(2):
        q = jnp.where(side == h, qt, jnp.zeros((), BF))
        scores = []
        top = None
        for i in range(4):
            rows = slice(part_keys * (i % 2), part_keys * (i % 2 + 1))
            bias = (bias0, bias1)[i // 2][2 * pair + h, rows, :]
            score = dot((own, other)[i // 2][0, rows, cols], q) + bias.astype(F32)
            high = jnp.max(score, axis=0, keepdims=True)
            top = high if i == 0 else jnp.maximum(top, high)
            scores.append(score)
        part = None
        for i, score in enumerate(scores):
            values = vts[i // 2][64 * h : 64 * h + 64, part_keys * (i % 2) : part_keys * (i % 2 + 1)]
            e = jnp.exp(score - top).astype(BF)
            piece = dot(jnp.concatenate([values, ones], axis=0), e)
            part = piece if i == 0 else part + piece
        total = part[64:65, :]
        lse_ref[pair, h : h + 1, :] = top + jnp.log(total)
        results.append(part[0:64, :] / total)
    full = jnp.concatenate(results, axis=0).T
    full_ref[:, cols] = full
    att_ref[:, cols] = full.astype(BF)


def attend(q, own, other, labels, table, begin, pairs, before, deps):
    rows, width = q.shape
    return call(
        partial(attend_kernel, begin),
        (q, own, other, labels, table, *before),
        [sds((rows, width), BF), sds((rows, width), F32), sds((width // 128, 2, rows), F32)],
        "attend",
        [VM] * (5 + len(before)),
        [VM] * 3,
        grid=(pairs,),
        deps=deps,
        aliases={5: 0, 6: 1, 7: 2} if before else None,
    )


def project_kernel(x_ref, att_ref, o_ref, gain, mid_ref, nf_ref):
    mid = x_ref[...].astype(F32) + dot(att_ref[...], o_ref[...])
    mid_ref[...] = mid
    scale = lax.rsqrt(jnp.mean(mid * mid, axis=-1, keepdims=True) + EPS)
    nf_ref[...] = (mid * scale * gain[...]).astype(BF)


def ffn_kernel(first_call, begin, place, nf_ref, g0, g1, g2, g3, mine, other, *refs):
    if first_call:
        out_ref, dnf_ref, keep, send, w1s, w2s, gs, us, ds = refs
    else:
        out_in, dnf_in = refs[:2]
        out_ref, dnf_ref, keep, send, w1s, w2s, gs, us, ds = refs[-9:]
    first = place[1] == 0
    step = pl.program_id(0)
    block = step + begin

    @pl.when(step == 0)
    def _():
        for r, ref in enumerate((g0, g1, g2, g3)):
            gs[128 * r : 128 * r + 128, :] = ref[...]
        if first_call:
            out_ref[...] = jnp.zeros_like(out_ref)
            dnf_ref[...] = jnp.zeros_like(dnf_ref)
        else:
            out_ref[...] = out_in[...]
            dnf_ref[...] = dnf_in[...]

    for s in range(4):
        rows = slice(192 * s, 192 * s + 192)
        for i, w in enumerate((w1s, w2s)):
            m = mine[place[2 + s], block, i]
            o = other[place[6 + s], block, i]
            w[rows, 0:384] = jnp.where(first, m, o)
            w[rows, 384:768] = jnp.where(first, o, m)
    for j in range(3):
        cols = slice(256 * j, 256 * j + 256)
        v = dot(nf_ref[...], w1s[:, cols])
        square = v * v
        th = jnp.tanh(v * (0.7978845608 + (0.7978845608 * 0.044715) * square))
        half = 0.5 + 0.5 * th
        us[:, cols] = (v * half).astype(BF)
        slope = half + v * (0.5 - 0.5 * th * th) * (0.7978845608 + (0.7978845608 * 3 * 0.044715) * square)
        ds[:, cols] = (dot(gs[...], w2s[cols, :], NT) * slope).astype(BF)
    out_ref[...] += dot(us[...], w2s[...])
    dnf_ref[...] += dot(ds[...], w1s[...], NT)
    d1 = dot(nf_ref[...], ds[...], TN).astype(BF)
    d2 = dot(us[...], gs[...], TN).astype(BF)
    for s in range(4):
        rows = slice(192 * s, 192 * s + 192)
        for i, d in enumerate((d1, d2)):
            lo = d[rows, 0:384]
            hi = d[rows, 384:768]
            keep[place[2 + s], block, i] = jnp.where(first, lo, hi)
            send[place[6 + s], block, i] = jnp.where(first, hi, lo)


def ffn_blocks(place, nf, g, mine, other, carry, grads, begin, count, deps):
    rows, width = nf.shape
    aliases = {}
    if carry:
        aliases = {8: 0, 9: 1}
    if grads:
        aliases.update({10: 2, 11: 3})
    return call(
        partial(ffn_kernel, not carry, begin),
        (place, nf, *g, mine, other, *carry, *grads),
        [sds((rows, width), F32), sds((rows, width), F32)] + [sds(mine.shape, BF)] * 2,
        "ffn",
        [SM] + [VM] * (7 + len(carry) + len(grads)),
        [VM] * 4,
        grid=(count,),
        scratch=[pltpu.VMEM((width, width), BF)] * 2 + [pltpu.VMEM((rows, width), BF)] * 3,
        deps=deps,
        aliases=aliases,
    )


def store_gain(ref, value):
    for i in range(ref.shape[0]):
        ref[i : i + 1, :] = value[:, 128 * i : 128 * i + 128]


def turn_kernel(mid_ref, out_in, dnf_in, g0, g1, g2, g3, gain, o_ref, full_ref, h0, h1, h2, h3, dmid_ref, dml_ref, da_ref, delta_ref, gg_ref):
    mid = mid_ref[...]
    hid = (mid + out_in[...]).astype(BF)
    for r, ref in enumerate((h0, h1, h2, h3)):
        ref[...] = hid[128 * r : 128 * r + 128, :]
    scale = lax.rsqrt(jnp.mean(mid * mid, axis=-1, keepdims=True) + EPS)
    up = dnf_in[...]
    weighted = up * gain[...]
    mean_term = jnp.mean(weighted * mid, axis=-1, keepdims=True)
    res = scale * weighted - mid * (scale * scale * scale) * mean_term
    store_gain(gg_ref, jnp.sum(up * mid * scale, axis=0, keepdims=True))
    for r, ref in enumerate((g0, g1, g2, g3)):
        rows = slice(128 * r, 128 * r + 128)
        dmid_ref[rows, :] = res[rows, :] + ref[...].astype(F32)
    low = dmid_ref[...].astype(BF)
    dml_ref[...] = low
    da = dot(low, o_ref[...], NT).astype(BF)
    da_ref[...] = da
    pairs = delta_ref.shape[0]
    width = da.shape[1]
    head = lax.broadcasted_iota(jnp.int32, (2 * pairs, width), 0)
    lane = lax.broadcasted_iota(jnp.int32, (2 * pairs, width), 1)
    pick = jnp.where(lane // 64 == head, 1.0, 0.0)
    delta = lax.dot_general(
        pick, da.astype(F32) * full_ref[...], NT, precision=lax.Precision.HIGHEST, preferred_element_type=F32
    )
    for p in range(pairs):
        delta_ref[p] = delta[2 * p : 2 * p + 2, :]


def split_rows(value):
    row = lax.broadcasted_iota(jnp.int32, (64, value.shape[1]), 0)
    out = jnp.zeros((64, value.shape[1]), BF)
    for i in range(3):
        piece = value.astype(BF)
        out = jnp.where(row == i, piece, out)
        value = value - piece.astype(F32)
    return out


def attend_back_kernel(begin, half, last, q_ref, da_ref, kv_ref, labels, table, lse_ref, delta_ref, *refs):
    if last:
        dq_in, dq_ref, dkv_ref, ds_ref = refs
    else:
        dq_ref, dkv_ref, ds_ref = refs
    pair = pl.program_id(0) + begin
    cols = lanes_of(pair)
    outs = lanes_of(pl.program_id(0))
    part_keys = kv_ref.shape[1] // 2
    zero = jnp.zeros((), BF)
    q_all, da_all = q_ref[:, cols], da_ref[:, cols]
    qt = q_all.T
    dat = da_all.T
    kt = kv_ref[0, :, cols].T
    lane = lax.broadcasted_iota(jnp.int32, (1, 128), 1)
    dqs = [None, None]
    qs, das, qas, daas = [], [], [], []
    for h in range(2):
        own = lane // 64 == h
        qs.append(jnp.where(own, q_all, zero))
        das.append(jnp.where(own, da_all, zero))
        for t, stat, out in ((qt, lse_ref, qas), (dat, delta_ref, daas)):
            extra = split_rows(stat[pair, h : h + 1, :])
            mine = t[64 * h : 64 * h + 64, :]
            out.append(jnp.concatenate([mine, extra] if h == 0 else [extra, mine], axis=0))
    for i in range(2):
        rows = slice(part_keys * i, part_keys * (i + 1))
        k = kv_ref[0, rows, cols]
        v = kv_ref[1, rows, cols]
        dk = dv = None
        for h in range(2):
            own = lane // 64 == h
            minus = jnp.where(lane % 64 < 3, -1.0, 0.0).astype(BF)
            first = half * kv_ref.shape[1] + part_keys * i
            bias = look_up(table, 2 * pair + h, labels[first : first + part_keys, :])
            p = jnp.exp(dot(jnp.where(own, k, minus), qas[h]) + bias)
            ds = (p * dot(jnp.where(own, v, minus), daas[h])).astype(BF)
            ds_ref[2 * pl.program_id(0) + h, rows, :] = ds
            a = dot(kt[64 * h : 64 * h + 64, rows], ds)
            b = dot(ds, qs[h])
            c = dot(p.astype(BF), das[h])
            dqs[h] = a if i == 0 else dqs[h] + a
            dk, dv = (b, c) if h == 0 else (dk + b, dv + c)
        dkv_ref[0, rows, outs] = dk.astype(dkv_ref.dtype)
        dkv_ref[1, rows, outs] = dv.astype(dkv_ref.dtype)
    dq = jnp.concatenate(dqs, axis=0).T
    if last:
        dq_ref[:, outs] = (dq_in[:, outs] + dq).astype(dq_ref.dtype)
    else:
        dq_ref[:, outs] = dq


def attend_back(q, da, kv, labels, table, half, begin, pairs, lse, delta, dq, deps):
    rows = q.shape[0]
    width = 128 * pairs
    keys = kv.shape[1]
    last = len(dq) > 0
    return call(
        partial(attend_back_kernel, begin, half, last),
        (q, da, kv, labels, table, lse, delta, *dq),
        [
            sds((rows, width), BF if last else F32),
            sds((2, keys, width), F32 if last else BF),
            sds((2 * pairs, keys, rows), BF),
        ],
        "attend_back",
        [VM] * (7 + len(dq)),
        [VM] * 3,
        grid=(pairs,),
        deps=deps,
    )


def weights_kernel(blocks, last, place, xn_ref, dq_ref, dkv_in, dkv_add, a_ref, att_ref, dml_ref, *refs):
    if last:
        up_in, dmid_ref, x_ref, gain, keep, send, h0, h1, h2, h3, gg_ref = refs
        up = up_in[...]
    else:
        keep, send, up_ref = refs
        up = None
    first = place[1] == 0
    dq = dq_ref[...]
    dk, dv = ((dkv_in[i] + dkv_add[i].astype(F32)).astype(BF) for i in range(2))
    xn = xn_ref[...]
    for i, k in enumerate(blocks):
        cols = slice(192 * i, 192 * i + 192)
        cat = jnp.concatenate([dq[:, cols], dk[:, cols], dv[:, cols]], axis=1)
        part = dot(cat, a_ref[k, :, 0:576], NT)
        up = part if up is None else up + part
        grad = dot(xn, cat, TN).astype(BF)
        out = dot(att_ref[:, 192 * k : 192 * k + 192], dml_ref[...], TN).astype(BF)
        for s in range(4):
            rows = slice(192 * s, 192 * s + 192)
            lo = grad[rows, 0:384]
            piece = jnp.concatenate(
                [out[48 * s : 48 * s + 48, 192 * c : 192 * c + 192] for c in range(4)], axis=0
            )
            hi = jnp.concatenate([grad[rows, 384:576], piece], axis=1)
            keep[place[2 + s], i] = jnp.where(first, lo, hi)
            send[place[6 + s], i] = jnp.where(first, hi, lo)
    if not last:
        up_ref[...] = up
        return
    x = x_ref[...].astype(F32)
    scale = lax.rsqrt(jnp.mean(x * x, axis=-1, keepdims=True) + EPS)
    weighted = up * gain[...]
    mean_term = jnp.mean(weighted * x, axis=-1, keepdims=True)
    res = scale * weighted - x * (scale * scale * scale) * mean_term
    store_gain(gg_ref, jnp.sum(up * x * scale, axis=0, keepdims=True))
    back = (dmid_ref[...] + res).astype(BF)
    for r, ref in enumerate((h0, h1, h2, h3)):
        ref[...] = back[128 * r : 128 * r + 128, :]


def place_kernel(place, mine, other, q_out, k_out, v_out, o_out):
    first = place[1] == 0
    lo = jnp.where(first, mine[...], other[...]).astype(F32)
    hi = jnp.where(first, other[...], mine[...]).astype(F32)
    q_out[...] = lo[:, 0:192]
    k_out[...] = lo[:, 192:384]
    v_out[...] = hi[:, 0:192]
    for i in range(4):
        o_out[:, 192 * i : 192 * i + 192] = hi[48 * i : 48 * i + 48, 192:384]


def bucket_kernel(source, adds, place, labels, ds0_ref, ds1_ref, *refs):
    before = refs[0] if adds else None
    out_ref, acc, table = refs[-3:]
    tp = place[0]
    step = pl.program_id(0)
    heads, _, queries = ds0_ref.shape
    group = 128
    first = source * (labels.shape[0] // 2) + step * group

    @pl.when(step == 0)
    def _():
        acc[...] = jnp.zeros_like(acc)

    label = [(lax.broadcasted_iota(jnp.int32, (16, 128), 0) + 16 * i).astype(F32).astype(BF) for i in range(2)]
    one, zero = jnp.ones((), BF), jnp.zeros((), BF)
    for g in range(group // 16):
        for k in range(queries // 128):
            index = labels[pl.ds(pl.multiple_of(first + 16 * g, 16), 16), 128 * k : 128 * k + 128].astype(F32)
            for j in range(16):
                spread = jnp.broadcast_to(index[j : j + 1, :], (16, 128)).astype(BF)
                for i in range(2):
                    at = 32 * j + 16 * i
                    table[at : at + 16, 128 * k : 128 * k + 128] = jnp.where(spread == label[i], one, zero)
        part = pl.ds(pl.multiple_of(step * group + 16 * g, 16), 16)
        left = [d[:, part, :].reshape(heads * 16, queries) for d in (ds0_ref, ds1_ref)]
        acc[...] += dot(jnp.concatenate(left, axis=0), table[...], NT)

    @pl.when(step == pl.num_programs(0) - 1)
    def _():
        row = lax.broadcasted_iota(jnp.int32, acc.shape, 0) % 16
        col = lax.broadcasted_iota(jnp.int32, acc.shape, 1) // 32
        hit = jnp.where(row == col, acc[...], 0.0)
        fold = (hit[:, 0:128] + hit[:, 128:256]) + (hit[:, 256:384] + hit[:, 384:512])
        sums = jnp.sum(fold.reshape(2 * heads, 16, 128), axis=1)
        sums = sums + pltpu.roll(sums, 64, 1)
        sums = sums + pltpu.roll(sums, 32, 1)
        lane = lax.broadcasted_iota(jnp.int32, sums.shape, 1)
        sums = jnp.where(lane < 32, sums, 0.0)
        out_ref[...] = jnp.zeros_like(out_ref) if before is None else before[...]
        each = heads // 2
        for k in range(4):
            for h in range(each):
                at = (tp ^ ORDER[k]) * each + h
                out_ref[pl.ds(at, 1), :] = out_ref[pl.ds(at, 1), :] + sums[each * k + h : each * k + h + 1, :]


def bucket_sums(place, half, labels, ds, before, deps):
    heads, keys, queries = ds[0].shape
    return call(
        partial(bucket_kernel, half, len(before)),
        (place, labels, ds[0], ds[1], *before),
        [sds((16, 128), F32)],
        "bucket_sums",
        [SM] + [VM] * (3 + len(before)),
        [VM],
        grid=(keys // 128,),
        scratch=[pltpu.VMEM((heads * 32, 512), F32), pltpu.VMEM((512, queries), BF)],
        deps=deps,
    )


def move(value, move_to, sizes):
    shards, ctx, tps = sizes
    pairs = []
    for s in range(shards):
        for c in range(ctx):
            for t in range(tps):
                a, b, d = move_to(s, c, t)
                pairs.append(((s * ctx + c) * tps + t, (a * ctx + b) * tps + d))
    return lax.ppermute(value, ALL, pairs)


def body(
    hidden_in,
    norm_attn_gain,
    query_weight,
    key_weight,
    value_weight,
    out_weight,
    bias_table,
    norm_ffn_gain,
    ffn_in_weight,
    ffn_out_weight,
    buckets,
    output_gradient,
):
    sizes = tuple(lax.axis_size(a) for a in ALL)
    shards, ctxs, tps = sizes
    s, c, t = (lax.axis_index(a) for a in ALL)
    fast = shards == 4
    assert ctxs == 2 and tps == 4 and hidden_in.shape[0] == tps
    heads = bias_table.shape[1]

    def along(k):
        return lambda a, b, d: (a, b, d ^ k)

    def across(a, b, d):
        return (a, 1 - b, d)

    def near(a, b, d):
        return (a ^ (1 if b == 0 else 2), b, d)

    def far(a, b, d):
        return (a ^ (2 if b == 0 else 1), b, d)

    go = partial(move, sizes=sizes)

    def spot(shard, core):
        d = shard ^ s
        return jnp.where(core == 0, d, (d >> 1) | ((d & 1) << 1)) if fast else jnp.int32(shard)

    place = jnp.stack(
        [t, c] + [spot(i, c) for i in range(4)] + [spot(i, 1 - c) for i in range(4)]
    ).astype(jnp.int32)

    def pick(value, k):
        return lax.dynamic_index_in_dim(value, t ^ k, 0, keepdims=False)

    def tie(value, token):
        return lax.optimization_barrier((value, token))

    def add(a, b):
        return (a.astype(F32) + b.astype(F32)).astype(BF)

    def send_near(value):
        return go(value, near) if fast else value

    def send_far(value):
        return go(value, far) if fast else value

    def join_near(value, got):
        return jnp.stack([value, got]) if fast else value

    def join_far(value, got):
        if fast:
            return jnp.concatenate([value, got])
        full = lax.all_gather(value, "shard", axis=0, tiled=False)
        full = jnp.moveaxis(full, 0, -3)
        lead = full.shape[:-3]
        return jnp.moveaxis(full.reshape(lead + (4, 192, 384)), -3, 0)

    def stage_far(keep, got):
        if fast:
            return add(keep[:2], got[:2]), add(keep[2:], got[2:])
        return add(keep, got), jnp.zeros((8, 128), BF)

    def stage_near(stay, got):
        return (add(stay[0], got[0]), add(stay[1], got[1])) if fast else (stay, got)

    def stage_last(stay, got):
        if fast:
            return [add(stay[i], got[i]) for i in range(stay.shape[0])]
        total = jnp.moveaxis(stay, 0, -3)
        lead = total.shape[:-3]
        total = jnp.moveaxis(total.reshape(lead + (shards, 768 // shards, 384)), -3, 0)
        total = lax.psum_scatter(total, "shard", scatter_dimension=0, tiled=False)
        return [total[i] for i in range(total.shape[0])]

    def my_half(lo, hi):
        return jnp.where(c == 0, lo, hi)

    def both_halves(mine, other):
        return jnp.where(c == 0, mine, other).astype(F32), jnp.where(c == 0, other, mine).astype(F32)

    width = hidden_in.shape[2]
    n = 512
    ga = norm_attn_gain.reshape(1, width)
    gf = norm_ffn_gain.reshape(1, width)
    row = sds((n, width), BF)
    out_rows = out_weight.shape[0]

    out_pack = jnp.concatenate([out_weight[:, 192 * i : 192 * i + 192] for i in range(4)], axis=0)
    att_half = my_half(
        jnp.concatenate([query_weight, key_weight], axis=1), jnp.concatenate([value_weight, out_pack], axis=1)
    )
    ffn_half = my_half(
        jnp.stack([ffn_in_weight[:, :384], ffn_out_weight[:, :384]]),
        jnp.stack([ffn_in_weight[:, 384:], ffn_out_weight[:, 384:]]),
    )
    head_order = jnp.concatenate([(t ^ k) * (heads // tps) + jnp.arange(heads // tps) for k in ORDER])
    table_rel = jnp.pad(jnp.take(bias_table.T, head_order, axis=0), ((0, 0), (0, 128 - bias_table.shape[0])))

    def both(value, token):
        return lax.optimization_barrier((value, token))

    pair = jnp.stack([att_half, go(att_half, along(2))])
    a0 = go(pair, along(1))
    own = send_near(ffn_half)
    own, pair = both(own, pair)
    own = join_near(ffn_half, own)
    own_m = send_far(own)
    xs = [pick(hidden_in, k) for k in range(tps)]
    labels, tok = order_buckets(place, buckets, [pair, own, *xs])
    (a0, own_m), tok = tie((a0, own_m), tok)
    own_m = join_far(own, own_m)
    a0 = jnp.concatenate([pair, a0])
    a1 = send_near(a0)
    ffn_w, a0 = both(ffn_half, a0)
    w2 = go(ffn_w, along(2))
    tok = fence(tok, a0, ffn_w)
    a1, tok = tie(a1, tok)
    a1 = join_near(a0, a1)
    am = send_far(a1)
    xs, a1 = both(xs, a1)
    zx = [go(xs[k], along(k)) for k in (1, 2, 3)]
    bias = [None] * 2
    bias[0], tok = position_bias(labels, table_rel, 0, [tok, a1, *xs])
    am, tok = tie(am, tok)
    am = join_far(a1, am)
    ao = go(am, across)
    w2, am = both(w2, am)
    pan = send_near(w2)
    bias[1], tok = position_bias(labels, table_rel, 1, [tok, am, w2])
    (ao, zx), tok = tie((ao, zx), tok)
    pair_w = jnp.stack([ffn_half, w2])
    pair_w, zx = both(pair_w, zx)
    pb = go(pair_w, along(1))
    x_parts = [xs[0]] + zx
    if not fast:
        def regroup(z):
            part = z[..., 192:].reshape(4, 4, shards // 4, 4, out_rows, 192)
            part = jnp.transpose(part, (0, 1, 3, 2, 4, 5)).reshape(4, 4, 192, 192)
            return jnp.concatenate([z[..., :192], part], axis=-1)

        fixed_m, fixed_o = regroup(am), regroup(ao)
        am, ao = jnp.where(c == 1, fixed_m, am), jnp.where(c == 0, fixed_o, ao)

    x, xn, q, kv, a_full, o_full, tok = call(
        qkv_kernel,
        (place, *x_parts, ga, am, ao),
        [row, row, row, sds((2, n, width), BF), sds((4, width, width), BF), sds((width, width), BF)],
        "qkv",
        [SM] + [VM] * 7,
        [VM] * 6,
        deps=[tok, pair_w],
    )
    kv_other = go(kv, across)
    tok = mark(tok, kv)
    pan, tok = tie(pan, tok)
    pa = join_near(w2, pan)
    pam = send_far(pa)
    tok = fence(tok, pa)
    kv_other, tok = tie(kv_other, tok)
    att, full, lse, tok = attend(q, kv, kv_other, *bias, 0, 4, (), [tok])
    pb, tok = tie(pb, tok)
    pbn = send_near(pb)
    tok = mark(tok, pb)
    gs, tok = tie([pick(output_gradient, kk) for kk in range(tps)], tok)
    zg = {kk: go(gs[kk], along(kk)) for kk in (1, 2, 3)}
    att, full, lse, tok = attend(q, kv, kv_other, *bias, 4, 2, (att, full, lse), [tok, *gs])
    (pam, pbn), tok = tie((pam, pbn), tok)
    pam = jnp.stack([own_m, join_far(pa, pam)], axis=1)
    pao = go(pam, across)
    pb = join_near(pb, pbn)
    pbm = send_far(pb)
    mid, nf, tok = call(
        project_kernel,
        (x, att, o_full, gf),
        [sds((n, width), F32), row],
        "project",
        [VM] * 4,
        [VM] * 2,
        deps=[tok, pam, pb],
    )
    (zg, pao), tok = tie((zg, pao), tok)
    g_parts = [gs[0]] + [zg[kk] for kk in (1, 2, 3)]

    out_acc, dnf, keep_a, send_a, tok = ffn_blocks(place, nf, g_parts, pam, pao, (), (), 0, 2, [tok])
    cross_a = go(send_a, across)
    pbm, tok = tie(pbm, tok)
    pbm = join_far(pb, pbm)
    pbo = go(pbm, across)
    tok = fence(tok, pbm, send_a)
    pbo, tok = tie(pbo, tok)
    out_acc, dnf, keep_b, send_b, tok = ffn_blocks(
        place, nf, g_parts, pbm, pbo, (out_acc, dnf), (), 0, 1, [tok, send_a]
    )
    cross_a, tok = tie(cross_a, tok)
    stay_a, leave_a = stage_far(keep_a, cross_a)
    far_a = send_far(leave_a)
    out_acc, dnf, keep_b, send_b, tok = ffn_blocks(
        place, nf, g_parts, pbm, pbo, (out_acc, dnf), (keep_b, send_b), 1, 1, [tok, stay_a, leave_a]
    )
    cross_b = go(send_b, across)

    piece = sds((n // tps, width), BF)
    gain_rows = sds((width // 128, 128), F32)
    *hids, dmid, dml, da, delta, gf_grad, tok = call(
        turn_kernel,
        (mid, out_acc, dnf, *g_parts, gf, o_full, full),
        [piece] * 4 + [sds((n, width), F32), row, row, sds((heads // 2, 2, n), F32), gain_rows],
        "turn",
        [VM] * 10,
        [VM] * 9,
        deps=[tok, send_b],
    )

    def arrange(pieces):
        stacked = jnp.stack(pieces)
        return jnp.stack([pick(stacked, i) for i in range(tps)])

    hid_parts = [go(hids[k], along(k)) for k in (1, 2, 3)]
    (cross_b, far_a), tok = tie((cross_b, far_a), tok)
    stay_a, leave_a = stage_near(stay_a, far_a)
    near_a = send_near(leave_a)
    stay_b, leave_b = stage_far(keep_b, cross_b)
    far_b = send_far(leave_b)
    dq1, dkv1, ds11, tok = attend_back(
        q, da, kv_other, labels, table_rel, 1, 3, 3, lse, delta, (), [tok, stay_b, leave_b, stay_a, leave_a, *hids]
    )
    dkv1 = go(dkv1, across)
    first_hids, tok = tie(hid_parts[:2], tok)
    hid_parts = [*first_hids, hid_parts[2]]
    dq1, own1, ds01, tok = attend_back(
        q, da, kv, labels, table_rel, 0, 3, 3, lse, delta, (dq1,), [tok]
    )
    (near_a, far_b, dkv1, hid_parts[2]), tok = tie((near_a, far_b, dkv1, hid_parts[2]), tok)
    blocks_a = stage_last(stay_a, near_a)
    stay_b, leave_b = stage_near(stay_b, far_b)
    near_b = send_near(leave_b)

    keep_v, send_v, up, tok = call(
        partial(weights_kernel, (2, 3), False),
        (place, xn, dq1, own1, dkv1, a_full, att, dml),
        [sds((4, 2, 192, 384), BF), sds((4, 2, 192, 384), BF), sds((n, width), F32)],
        "weights",
        [SM] + [VM] * 7,
        [VM] * 3,
        deps=[tok, stay_b, leave_b, *blocks_a, *hid_parts],
    )
    if not fast:
        def ungroup(z):
            part = z[..., 192:].reshape(4, 2, 4, shards // 4, out_rows, 192)
            part = jnp.transpose(part, (0, 1, 3, 2, 4, 5)).reshape(4, 2, 192, 192)
            return jnp.concatenate([z[..., :192], part], axis=-1)

        def ungroup_both(keep, send):
            return jnp.where(c == 1, ungroup(keep), keep), jnp.where(c == 0, ungroup(send), send)

        keep_v, send_v = ungroup_both(keep_v, send_v)
    cross_v = go(send_v, across)
    near_b, tok = tie(near_b, tok)
    blocks_b = jnp.stack(stage_last(stay_b, near_b))
    zb = go(blocks_b, along(1))
    dq0, dkv0, ds10, tok = attend_back(
        q, da, kv_other, labels, table_rel, 1, 0, 3, lse, delta, (), [tok, send_v, blocks_b]
    )
    dkv0 = go(dkv0, across)
    cross_v, tok = tie(cross_v, tok)
    stay_v, leave_v = stage_far(keep_v, cross_v)
    far_v = send_far(leave_v)
    dq0, own0, ds00, tok = attend_back(
        q, da, kv, labels, table_rel, 0, 0, 3, lse, delta, (dq0,), [tok, stay_v, leave_v]
    )
    (far_v, dkv0, zb), tok = tie((far_v, dkv0, zb), tok)
    c0, c2 = add(blocks_a[0], zb[0]), add(blocks_a[1], zb[1])
    zc = go(c2, along(2))
    stay_v, leave_v = stage_near(stay_v, far_v)
    near_v = send_near(leave_v)
    sums, tok = bucket_sums(place, 1, labels, (ds10, ds11), (), [tok, stay_v, leave_v, dkv0, c0, c2])
    near_v, tok = tie(near_v, tok)
    blocks_v = jnp.stack(stage_last(stay_v, near_v))
    zv = go(blocks_v, along(1))
    keep_w, send_w, *backs, ga_grad, tok = call(
        partial(weights_kernel, (0, 1), True),
        (place, xn, dq0, own0, dkv0, a_full, att, dml, up, dmid, x, ga),
        [sds((4, 2, 192, 384), BF)] * 2 + [piece] * 4 + [gain_rows],
        "weights",
        [SM] + [VM] * 11,
        [VM] * 7,
        deps=[tok, blocks_v],
    )
    if not fast:
        keep_w, send_w = ungroup_both(keep_w, send_w)
    cross_w = go(send_w, across)
    zc, tok = tie(zc, tok)
    ffn_mine = add(c0, zc)
    back_parts = [backs[0]] + [go(backs[k], along(k)) for k in (1, 2)]
    tok = fence(tok, backs, send_w, ffn_mine)
    cross_w, tok = tie(cross_w, tok)
    stay_w, leave_w = stage_far(keep_w, cross_w)
    far_w = send_far(leave_w)
    sums, tok = bucket_sums(place, 0, labels, (ds00, ds01), (sums,), [tok, stay_w, leave_w])
    (far_w, zv, got_backs), tok = tie((far_w, zv, back_parts), tok)
    ffn_mine, zv = both(ffn_mine, zv)
    ffn_other = go(ffn_mine, across)
    stay_w, leave_w = stage_near(stay_w, far_w)
    near_w = send_near(leave_w)
    back3 = go(backs[3], along(3))
    small = jnp.concatenate([sums, jnp.pad(ga_grad, ((0, 2), (0, 0))), jnp.pad(gf_grad, ((0, 2), (0, 0)))])
    got = go(small, across)
    tok = fence(tok, stay_w, leave_w, small, ffn_mine)
    (got, ffn_other), tok = tie((got, ffn_other), tok)
    small = small + got
    ffn_lo, ffn_hi = both_halves(ffn_mine, ffn_other)
    if fast:
        got = go(small, lambda a, b, d: (a ^ 1, b, d))
        tok = fence(tok, small)
        (got, near_w), tok = tie((got, near_w), tok)
        small = small + got
        got = go(small, lambda a, b, d: (a ^ 2, b, d))
    else:
        small = lax.psum(small, "shard")
    blocks_w = stage_last(stay_w, near_w)
    d0, d2 = add(blocks_w[0], zv[0]), add(blocks_w[1], zv[1])
    zw = go(d2, along(2))
    w1_grad = jnp.concatenate([ffn_lo[0], ffn_hi[0]], axis=1)
    w2_grad = jnp.concatenate([ffn_lo[1], ffn_hi[1]], axis=1)
    tok = fence(tok, small, d0, d2, w1_grad, w2_grad)
    if fast:
        got, tok = tie(got, tok)
        small = small + got
    got = go(small, along(1))
    tok = fence(tok, small)
    (got, zw, back3), tok = tie((got, zw, back3), tok)
    small = small + got
    got = go(small, along(2))
    att_mine = add(d0, zw)
    att_other = go(att_mine, across)
    hidden_grad = arrange([*got_backs, back3]).astype(F32)
    tok = fence(tok, small, att_mine, hidden_grad)
    (got, att_other), tok = tie((got, att_other), tok)
    small = small + got
    hidden_out = arrange([hids[0]] + hid_parts)
    table_grad = small[:heads, : bias_table.shape[0]].T
    gains = width // 128

    if fast:
        part = sds((192, 192), F32)
        q_grad, k_grad, v_grad, out_grad, _ = call(
            place_kernel,
            (place, att_mine, att_other),
            [part, part, part, sds((out_rows, width), F32)],
            "place",
            [SM, VM, VM],
            [VM] * 4,
        )
    else:
        att_lo, att_hi = both_halves(att_mine, att_other)
        q_grad, k_grad, v_grad = att_lo[:, :192], att_lo[:, 192:], att_hi[:, :192]
        out_grad = jnp.concatenate([att_hi[out_rows * i : out_rows * i + out_rows, 192:] for i in range(4)], axis=1)
    return (
        hidden_out,
        hidden_grad,
        small[16 : 16 + gains].reshape(width),
        q_grad,
        k_grad,
        v_grad,
        out_grad,
        table_grad,
        small[24 : 24 + gains].reshape(width),
        w1_grad,
        w2_grad,
    )


def solution(mesh):
    rows = P("shard", ("ctx", "tp"), None)
    cols = P("shard", "tp")
    both = P(("tp", "shard"), None)
    return jax.shard_map(
        body,
        mesh=mesh,
        in_specs=(rows, P(), cols, cols, cols, both, P(), P(), cols, both, P("ctx", None), rows),
        out_specs=(rows, rows, P(), cols, cols, cols, both, P(), P(), cols, both),
        check_vma=False,
    )
```
